512 devices in a mesh: dp: 4 (over x), expert: 32 (over z, y_lo), tensor: 4 (over y_hi, core).
Axes of the slice: x: 4, y: 8 (y_hi: 2, y_lo: 4; y = y_hi * 4 + y_lo), z: 8, core: 2. Of those that a mesh axis runs over, the one named last changes fastest.
Arguments:
- tokens: bfloat16 [16384, 7168], P(('dp', 'expert'), 'tensor'), may hold values from -6 to 6
- expert_ids: int32 [16384, 2], P(('dp', 'expert')), may hold values from 0 to 31, all different within a row; in each aligned block of 128 rows (0 to 127, 128 to 255, ...) at most 12 rows name the same one
- gate_scores: bfloat16 [16384, 2], P(('dp', 'expert')), may hold values from 0.099609375 to 0.59765625
- weight_in: bfloat16 [32, 2, 7168, 1024], P('expert', None, 'tensor', 'dp'), may hold values from -0.0625 to 0.0625
- weight_out: bfloat16 [32, 1024, 7168], P('expert', 'dp', 'tensor'), may hold values from -0.1875 to 0.1875
Outputs:
- mixed: bfloat16 [16384, 7168], P(('dp', 'expert'), 'tensor')
The draws below stay inside these ranges and needn't reach their ends.
Inputs may be any that keep to these rules, and one draw needn't show every extreme that they name: `expert_ids`: each token names 2 different experts; among the 128 tokens of one index of dp and expert together (aligned blocks of rows) no expert is named more than 12 times, and in some blocks an expert is named exactly 12 times.
All inputs are finite; a program needn't handle non-finite values.
Results may differ from the reference program's by a relative error of at most 0.0071.
Values may be sent and summed in bfloat16 or wider, within the bound.
No kernel may reach another device: no remote copies, remote signals or barrier semaphores. Data moves between devices by JAX's collectives and lax.ppermute only.
A program may use at most 64 MiB of HBM per device.

```python
import math
import jax
import jax.numpy as jnp
import numpy as np
from jax import lax

D = 7168
FF = 1024
TOK_GRP = 128
TOP = 2
EXPERTS = 32
CAP = 12
TOKENS = 16384


def shard_levels(rng, dims, cuts, low, top_value):
    level = 1.0
    for position, shards_of in cuts:
        heights = jax.random.uniform(jax.random.fold_in(jax.random.fold_in(rng, 6), position), (shards_of,), jnp.float32, low / len(cuts), top_value / len(cuts))
        level = level * jnp.repeat(jnp.exp(heights), dims[position] // shards_of).reshape((-1,) + (1,) * (len(dims) - 1 - position))
    return level


def routed_block(own_key, own, number, rows, count, top, limit, lean):
    order = jax.random.permutation(own_key, count)
    crowded, usual = shares(count, rows * top, limit, lean, True), shares(count, rows * top, limit, lean, False)
    places = jnp.arange(count)

    def named(tallies, offset_by):
        used = int((tallies > 0).sum())
        fixed = max(1, used // 4)
        shifted = fixed + (places - fixed + offset_by * (used - fixed)) % max(1, count - fixed)
        return jnp.zeros((count,), jnp.int32).at[order[jnp.where(places < fixed, places, shifted)]].set(jnp.asarray(tallies, jnp.int32))

    tallies = jnp.where(number % 4 == 0, named(crowded, number // 4), named(usual, number - number // 4 - 1))
    mixed = jax.random.permutation(jax.random.fold_in(own, 3), count)
    giver, sink = mixed[0:count // 2 * 2:2], mixed[1:count // 2 * 2:2]
    slack = jnp.minimum(tallies[giver] - 1, limit - tallies[sink]) // 2
    slack = jnp.where((giver == order[0]) | (sink == order[0]) | (tallies[sink] == 0), 0, jnp.maximum(slack, 0))
    shifted = jax.random.randint(jax.random.fold_in(own, 4), (count // 2,), 0, 1 << 20) % (slack + 1)
    tallies = tallies.at[giver].add(-shifted).at[sink].add(shifted)
    members = jnp.searchsorted(jnp.cumsum(tallies), jnp.arange(rows * top), side="right").astype(jnp.int32)
    table = members.reshape(top, rows).T
    table = table[jax.random.permutation(jax.random.fold_in(own, 1), rows)]
    offset_by = jax.random.randint(jax.random.fold_in(own, 2), (rows, 1), 0, top)
    return jnp.take_along_axis(table, (jnp.arange(top)[None, :] + offset_by) % top, axis=1)


def shares(count, total, most, slope, full):
    portions = [(1 << 20) // math.isqrt(rank ** slope) + 1 for rank in range(1, count + 1)]
    largest = most if full else min(most, max(-(-total // count), total * portions[0] // sum(portions)))
    least = 1 if total - largest >= count - 1 else 0
    holding, spare = [largest] + [least] * (count - 1), total - largest - least * (count - 1)
    while spare > 0:
        movable = [i for i in range(1, count) if holding[i] < largest] or [i for i in range(1, count) if holding[i] < most]
        whole, budget = sum([portions[i] for i in movable]), spare
        for i in movable:
            more = min(most - holding[i], max(1, budget * portions[i] // whole), spare)
            holding[i] = holding[i] + more
            spare = spare - more
    return np.array(holding)


def noise(own_key, shape, width, limit, cuts=(), kind=jnp.bfloat16):
    drawn = width * jax.random.normal(own_key, shape, jnp.float32)
    if cuts:
        drawn = drawn * shard_levels(own_key, shape, cuts, -0.22, 0.18)
    return jnp.clip(drawn, -limit, limit).astype(kind)


def setup_inputs(seed: int = 0) -> dict:
    key_list = jax.random.split(jax.random.key(seed), 6)
    tokens = noise(key_list[0], (TOKENS, D), 1.0, 6.0, ((0, 128), (1, 4)))
    expert_ids_keys = jax.random.split(jax.random.fold_in(key_list[1], 1), TOKENS // TOK_GRP)
    expert_ids_turns = jax.random.permutation(jax.random.fold_in(key_list[1], 3), TOKENS // TOK_GRP)
    expert_ids = jax.vmap(lambda own, number: routed_block(jax.random.fold_in(key_list[1], 2), own, number, TOK_GRP, EXPERTS, TOP, CAP, 1))(expert_ids_keys, expert_ids_turns).reshape((TOKENS, TOP))
    gate_scores = jnp.clip(0.099609375 + 0.49804688 * jax.random.uniform(key_list[2], (TOKENS, TOP), jnp.float32) ** shard_levels(key_list[2], (TOKENS, TOP), ((0, 128),), -0.2, 0.2), 0.099609375, 0.59765625).astype(jnp.bfloat16)
    weight_in = noise(key_list[3], (EXPERTS, 2, D, FF), D ** -0.5, 0.0625, ((0, 32), (2, 4), (3, 4)))
    weight_out = noise(key_list[4], (EXPERTS, FF, D), FF ** -0.5, 0.1875, ((0, 32), (1, 4), (2, 4)))
    return dict(tokens=tokens, expert_ids=expert_ids, gate_scores=gate_scores, weight_in=weight_in, weight_out=weight_out)


def reference(tokens, expert_ids, gate_scores, weight_in, weight_out):
    groups = TOKENS // TOK_GRP
    wide = tokens.astype(jnp.float32)
    mean_square = lax.optimization_barrier(jnp.mean(wide * wide, axis=1, keepdims=True))
    normed = (wide * lax.rsqrt(mean_square + 1e-06)).astype(jnp.bfloat16)
    grouped = normed.reshape(groups, TOK_GRP, D).astype(jnp.float32)
    flat_ids = expert_ids.reshape(groups, TOK_GRP * TOP)
    one_hot = (flat_ids[:, :, None] == jnp.arange(EXPERTS, dtype=jnp.int32)[None, None, :]).astype(jnp.int32)
    earlier = jnp.cumsum(one_hot, axis=1) - one_hot
    slot_pos = lax.optimization_barrier(jnp.sum(earlier * one_hot, axis=2)).astype(jnp.int32)
    slot_range = jnp.arange(CAP, dtype=jnp.int32)
    scores = gate_scores.astype(jnp.float32).reshape(groups, TOK_GRP, TOP, 1)

    def one_expert(totals, inputs):
        expert, gate_up, down = inputs
        matched = (flat_ids == expert)[:, :, None] & (slot_pos[:, :, None] == slot_range[None, None, :])
        matched = matched.astype(jnp.float32).reshape(groups, TOK_GRP, TOP, CAP)
        picked = lax.optimization_barrier(jnp.sum(matched, axis=2))
        gathered = jnp.einsum('gtc,gtd->gcd', picked, grouped).astype(jnp.bfloat16).reshape(groups * CAP, D)
        gate = jnp.dot(gathered, gate_up[0], preferred_element_type=jnp.float32)
        upward = jnp.dot(gathered, gate_up[1], preferred_element_type=jnp.float32)
        hidden = (jax.nn.silu(gate) * upward).astype(jnp.bfloat16)
        result = jnp.dot(hidden, down, preferred_element_type=jnp.float32).astype(jnp.bfloat16)
        result = result.reshape(groups, CAP, D).astype(jnp.float32)
        weights = lax.optimization_barrier(jnp.sum(matched * scores, axis=2))
        return (totals + jnp.einsum('gtc,gcd->gtd', weights, result), None)
    start_total = jnp.zeros((groups, TOK_GRP, D), jnp.float32)
    totals, unused = lax.scan(one_expert, start_total, (jnp.arange(EXPERTS, dtype=jnp.int32), weight_in, weight_out))
    return totals.reshape(TOKENS, D).astype(jnp.bfloat16)
```

```python
import functools

import jax
import jax.numpy as jnp
from jax import lax
from jax.experimental import pallas as pl
from jax.experimental.pallas import tpu as pltpu
from jax.sharding import Mesh
from jax.sharding import PartitionSpec as P

INTERPRET = False
BF = jnp.bfloat16
F32 = jnp.float32
TENSOR = ("yh", "core")
FULL, EXTRA = 8, 4
VM = pl.BlockSpec(memory_space=pltpu.VMEM)
SM = pl.BlockSpec(memory_space=pltpu.SMEM)
HBM = pl.BlockSpec(memory_space=pltpu.HBM)


def kernel_call(body, out_shape, in_specs, out_specs, scratch=(), flops=0, moved=0):
    return pl.pallas_call(
        body,
        out_shape=out_shape,
        in_specs=in_specs,
        out_specs=out_specs,
        scratch_shapes=list(scratch),
        cost_estimate=pl.CostEstimate(flops=flops, transcendentals=0, bytes_accessed=moved),
        compiler_params=pltpu.CompilerParams(vmem_limit_bytes=16 << 20),
        interpret=INTERPRET,
    )


def in_hbm(x):
    return x if INTERPRET else pltpu.with_memory_space_constraint(x, pltpu.HBM)


def dot(a, b):
    return jnp.dot(a, b, preferred_element_type=F32)


def iota(shape, dim):
    return lax.broadcasted_iota(jnp.int32, shape, dim)


def fold_rows(extra_rows, part):
    row, col = iota((extra_rows, 2 * extra_rows), 0), iota((extra_rows, 2 * extra_rows), 1)
    return ((row // EXTRA) * FULL + EXTRA * part + row % EXTRA == col).astype(F32).astype(BF)


def unfold_rows(extra_rows, part):
    row, col = iota((2 * extra_rows, extra_rows), 0), iota((2 * extra_rows, extra_rows), 1)
    return ((col // EXTRA) * FULL + EXTRA * part + col % EXTRA == row).astype(F32).astype(BF)


def pack_body(ids_ref, tok_ref, out_ref, *, experts):
    count, width = tok_ref.shape
    half = width // 2
    ids = ids_ref[...]
    named = [iota((experts, count), 0) == ids[k : k + 1, :] for k in range(2)]
    members = (named[0] | named[1]).astype(F32)
    before = (iota((count, count), 0) < iota((count, count), 1)).astype(F32)
    earlier = dot(members.astype(BF), before.astype(BF))
    place = iota((experts * FULL, count), 0)
    whole = jnp.zeros((experts * FULL, count), F32)
    low = jnp.zeros((experts * FULL, count), F32)
    high = jnp.zeros((experts * FULL, count), F32)
    for k in range(2):
        slot = jnp.sum(jnp.where(named[k], earlier, 0.0), axis=0, keepdims=True).astype(jnp.int32)
        base = ids[k : k + 1, :] * FULL
        far = base + slot - FULL
        whole += jnp.where((place == base + slot) & (slot < FULL), 1.0, 0.0)
        low += jnp.where((place == far) & (slot >= FULL), 1.0, 0.0)
        high += jnp.where((place == far + EXTRA) & (slot >= FULL), 1.0, 0.0)
    tok = tok_ref[...]
    out_ref[:, :width] = dot(whole.astype(BF), tok).astype(BF)
    folded = dot(low.astype(BF), tok[:, :half]) + dot(high.astype(BF), tok[:, half:])
    out_ref[:, width:] = folded.astype(BF)


def mix_body(ids_ref, score_ref, back_ref, out_ref, *, experts):
    count, width = out_ref.shape
    half = width // 2
    ids = ids_ref[...]
    score = score_ref[...].astype(F32)
    named = [iota((count, experts), 1) == ids[:, k : k + 1] for k in range(2)]
    members = (named[0] | named[1]).astype(F32)
    before = (iota((count, count), 1) < iota((count, count), 0)).astype(F32)
    earlier = dot(before.astype(BF), members.astype(BF))
    place = iota((count, experts * FULL), 1)
    whole = jnp.zeros((count, experts * FULL), F32)
    low = jnp.zeros((count, experts * FULL), F32)
    high = jnp.zeros((count, experts * FULL), F32)
    for k in range(2):
        slot = jnp.sum(jnp.where(named[k], earlier, 0.0), axis=1, keepdims=True).astype(jnp.int32)
        base = ids[:, k : k + 1] * FULL
        far = base + slot - FULL
        gain = score[:, k : k + 1]
        whole += jnp.where((place == base + slot) & (slot < FULL), gain, 0.0)
        low += jnp.where((place == far) & (slot >= FULL), gain, 0.0)
        high += jnp.where((place == far + EXTRA) & (slot >= FULL), gain, 0.0)
    whole, low, high = whole.astype(BF), low.astype(BF), high.astype(BF)
    folded = back_ref[:, width:]
    out_ref[:, :half] = (dot(whole, back_ref[:, :half]) + dot(low, folded)).astype(BF)
    out_ref[:, half:] = (dot(whole, back_ref[:, half:width]) + dot(high, folded)).astype(BF)


def split_in_two(total, lanes):
    big = total.astype(BF).astype(F32)
    return jnp.where(iota((total.shape[0], lanes), 1) < lanes // 2, big, total - big)


def first_body(where_ref, arrived_ref, *refs):
    weights, (send_ref, keep_ref, rows_ref, extra, wbuf, sems) = refs[:6], refs[6:]
    slots, width = rows_ref.shape
    quarter = slots // 4
    fulls, extras = quarter * 2 // 3, quarter // 3
    half = width // 2
    cols = wbuf.shape[2]
    copies = [pltpu.make_async_copy(w, wbuf.at[i], sems.at[i]) for i, w in enumerate(weights)]
    for copy in copies:
        copy.start()
    folded = arrived_ref[:, width:]
    extra[:, :half] = dot(fold_rows(4 * extras, 0), folded).astype(BF)
    extra[:, half:] = dot(fold_rows(4 * extras, 1), folded).astype(BF)
    core, yh = where_ref[0], where_ref[1]
    for q in range(4):
        core_q = 1 - core if q < 2 else core
        yh_q = 1 - yh if q % 2 == 0 else yh
        owner = yh_q * 2 + core_q
        at = q * quarter
        rows_ref[at : at + fulls, :] = arrived_ref[pl.ds(pl.multiple_of(owner * fulls, fulls), fulls), :width]
        rows_ref[at + fulls : at + quarter, :] = extra[pl.ds(pl.multiple_of(owner * extras, extras), extras), :]
    middle = slots // 2
    for first, out_ref in ((0, send_ref), (middle, keep_ref)):
        part = rows_ref[first : first + middle, :].astype(F32)
        squares = jnp.sum(part * part, axis=1, keepdims=True)
        lanes = out_ref.shape[1] - 6 * cols
        out_ref[:, 6 * cols :] = split_in_two(squares, lanes).astype(out_ref.dtype)
    for i, copy in enumerate(copies):
        copy.wait()
        at = i * cols
        send_ref[:, at : at + cols] = dot(rows_ref[:middle, :], wbuf[i]).astype(BF)
        keep_ref[:, at : at + cols] = dot(rows_ref[middle:, :], wbuf[i])


def last_body(rows_ref, wg_ref, wu_ref, send_ref, keep_ref):
    middle = rows_ref.shape[0] // 2
    cols = wg_ref.shape[1]
    for g, w in enumerate((wg_ref, wu_ref)):
        send_ref[:, g * cols : (g + 1) * cols] = dot(rows_ref[:middle, :], w[...]).astype(BF)
        keep_ref[:, g * cols : (g + 1) * cols] = dot(rows_ref[middle:, :], w[...])


def halve_body(keep_ref, got_ref, send_ref, own_ref, *, lanes):
    part, total = send_ref.shape
    sums = total - lanes
    send_ref[:, :sums] = (keep_ref[:part, :sums] + got_ref[:part, :sums].astype(F32)).astype(BF)
    own_ref[:, :sums] = keep_ref[part:, :sums] + got_ref[part:, :sums].astype(F32)
    if lanes:
        pair = keep_ref[:, sums:] + got_ref[:, sums:].astype(F32)
        both = pair[:, :1] + pair[:, lanes // 2 : lanes // 2 + 1]
        split = split_in_two(both, lanes)
        send_ref[:, sums:] = split[:part].astype(BF)
        own_ref[:, sums:] = split[part:]


def silu_times(gate, up):
    return gate / (1.0 + jnp.exp(-gate)) * up


def act_first_body(own_ref, got_ref, hid_ref, scale_ref, *, width_all):
    lanes = scale_ref.shape[1]
    sums = own_ref.shape[1] - lanes
    cols = sums // 6
    pair = own_ref[:, sums:] + got_ref[:, sums:].astype(F32)
    squares = pair[:, :1] + pair[:, lanes // 2 : lanes // 2 + 1]
    scale = lax.rsqrt(squares * (1.0 / width_all) + 1e-06)
    scale_ref[...] = jnp.broadcast_to(scale, scale_ref.shape)
    for i in range(3):
        at = 2 * i * cols
        both = (own_ref[:, at : at + 2 * cols] + got_ref[:, at : at + 2 * cols].astype(F32)) * scale
        hid_ref[:, i * cols : (i + 1) * cols] = silu_times(both[:, :cols], both[:, cols:]).astype(BF)


def act_last_body(own_ref, got_ref, early_ref, scale_ref, hid_ref):
    cols = own_ref.shape[1] // 2
    both = (own_ref[...] + got_ref[...].astype(F32)) * scale_ref[:, :1]
    hid_ref[:, : 3 * cols] = early_ref[...]
    hid_ref[:, 3 * cols :] = silu_times(both[:, :cols], both[:, cols:]).astype(BF)


def down_body(where_ref, hid_ref, w_ref, out_ref, ha, hb, wbuf, sems):
    chunks, cols, width = w_ref.shape
    half = width // 2
    me = where_ref[2]
    copies = []
    for i, step in enumerate((0, 3, 1, 2)):
        source = lax.rem(me + step, 4)
        copies.append(pltpu.make_async_copy(w_ref.at[source], wbuf.at[pl.ds(i * cols, cols)], sems.at[i]))
    for copy in copies:
        copy.start()
    quarter = hid_ref.shape[0] // 4
    fulls, extras = quarter * 2 // 3, quarter // 3
    for t in range(4):
        ha[t * fulls : (t + 1) * fulls, :] = hid_ref[t * quarter : t * quarter + fulls, :]
        hb[t * extras : (t + 1) * extras, :] = hid_ref[t * quarter + fulls : (t + 1) * quarter, :]
    low = dot(unfold_rows(4 * extras, 0), hb[...]).astype(BF)
    high = dot(unfold_rows(4 * extras, 1), hb[...]).astype(BF)
    for copy in copies:
        copy.wait()
    out_ref[:, :width] = dot(ha[...], wbuf[...]).astype(BF)
    folded = dot(low, wbuf[:, :half]) + dot(high, wbuf[:, half:])
    out_ref[:, width:] = folded.astype(BF)


def shape(*dims, dtype=BF):
    return jax.ShapeDtypeStruct(dims, dtype)


def per_device(tokens, expert_ids, gate_scores, weight_in, weight_out):
    experts = lax.axis_size("z") * lax.axis_size("yl")
    count, width = tokens.shape
    width_all = width * lax.axis_size(TENSOR)
    cols = weight_in.shape[3]
    wire = width + width // 2
    slots = experts * (FULL + EXTRA)
    half, part = slots // 2, slots // 4
    lanes = 128
    first_cols = 6 * cols + lanes
    right = [(i, (i + 1) % 4) for i in range(4)]
    left = [(i, (i - 1) % 4) for i in range(4)]
    swap = [(0, 1), (1, 0)]
    where = jnp.stack([lax.axis_index("core"), lax.axis_index("yh"), lax.axis_index("dp")]).astype(jnp.int32)

    own_gate, own_up = weight_in[0, 0], weight_in[0, 1]
    left_gate = lax.ppermute(own_gate, "dp", right)
    right_up = lax.ppermute(own_up, "dp", left)
    left_up = lax.ppermute(own_up, "dp", right)
    right_gate = lax.ppermute(own_gate, "dp", left)
    far_gate = lax.ppermute(left_gate, "dp", right)
    far_up = lax.ppermute(right_up, "dp", left)

    outgoing = kernel_call(
        functools.partial(pack_body, experts=experts),
        shape(experts * FULL, wire),
        [VM, VM],
        VM,
        flops=4 * experts * FULL * count * width,
        moved=4 << 20,
    )(expert_ids.T, tokens)
    arrived = lax.all_to_all(outgoing.reshape(experts, FULL, wire), ("z", "yl"), 0, 0, tiled=True)
    arrived = arrived.reshape(experts * FULL, wire)

    send, keep, rows = kernel_call(
        first_body,
        (shape(half, first_cols), shape(half, first_cols, dtype=F32), shape(slots, width)),
        [SM, VM] + [HBM] * 6,
        (VM, VM, VM),
        (
            pltpu.VMEM((experts * EXTRA, width), BF),
            pltpu.VMEM((6, width, cols), BF),
            pltpu.SemaphoreType.DMA((6,)),
        ),
        flops=12 * slots * width * cols,
        moved=12 << 20,
    )(where, arrived, *map(in_hbm, (own_gate, own_up, left_gate, left_up, right_gate, right_up)))
    got = lax.ppermute(send, "core", swap)
    send, keep = kernel_call(
        functools.partial(halve_body, lanes=lanes),
        (shape(part, first_cols), shape(part, first_cols, dtype=F32)),
        [VM, VM],
        (VM, VM),
        moved=3 << 20,
    )(keep, got)
    got = lax.ppermute(send, "yh", swap)
    early, scale = kernel_call(
        functools.partial(act_first_body, width_all=width_all),
        (shape(part, 3 * cols), shape(part, lanes, dtype=F32)),
        [VM, VM],
        (VM, VM),
        moved=1 << 20,
    )(keep, got)

    send, keep = kernel_call(
        last_body,
        (shape(half, 2 * cols), shape(half, 2 * cols, dtype=F32)),
        [VM, VM, VM],
        (VM, VM),
        flops=4 * slots * width * cols,
        moved=4 << 20,
    )(rows, far_gate, far_up)
    got = lax.ppermute(send, "core", swap)
    send, keep = kernel_call(
        functools.partial(halve_body, lanes=0),
        (shape(part, 2 * cols), shape(part, 2 * cols, dtype=F32)),
        [VM, VM],
        (VM, VM),
        moved=1 << 20,
    )(keep, got)
    got = lax.ppermute(send, "yh", swap)
    hidden = kernel_call(
        act_last_body, shape(part, 4 * cols), [VM, VM, VM, VM], VM, moved=1 << 20
    )(keep, got, early, scale)

    hidden = lax.all_gather(hidden, TENSOR, axis=0, tiled=True)
    own_out = weight_out[0] + sum(x[:1, :1] for x in (arrived, left_gate, right_up, left_up, right_gate)) * 0
    down = lax.all_gather(own_out, "dp", axis=0)
    sending = kernel_call(
        down_body,
        shape(experts * FULL, wire),
        [SM, VM, HBM],
        VM,
        (
            pltpu.VMEM((experts * FULL, 4 * cols), BF),
            pltpu.VMEM((experts * EXTRA, 4 * cols), BF),
            pltpu.VMEM((4 * cols, width), BF),
            pltpu.SemaphoreType.DMA((4,)),
        ),
        flops=4 * experts * FULL * 4 * cols * width,
        moved=6 << 20,
    )(where, hidden, in_hbm(down))
    back = lax.all_to_all(sending.reshape(experts, FULL, wire), ("z", "yl"), 0, 0, tiled=True)
    return kernel_call(
        functools.partial(mix_body, experts=experts),
        shape(count, width),
        [VM, VM, VM],
        VM,
        flops=4 * experts * FULL * count * width,
        moved=2 << 20,
    )(expert_ids, gate_scores, back.reshape(experts * FULL, wire))


def solution(mesh):
    dp, expert = mesh.shape["dp"], mesh.shape["expert"]
    finer = Mesh(mesh.devices.reshape(dp, expert // 4, 4, 2, 2), ("dp", "z", "yl", "yh", "core"))
    group = ("dp", "z", "yl")
    placed = (
        P(group, TENSOR),
        P(group, None),
        P(group, None),
        P(("z", "yl"), None, TENSOR, "dp"),
        P(("z", "yl"), "dp", TENSOR),
    )
    return jax.shard_map(
        per_device, mesh=finer, in_specs=placed, out_specs=P(group, TENSOR), check_vma=False
    )
```

```python
import functools

import jax
import jax.numpy as jnp
from jax import lax
from jax.experimental import pallas as pl
from jax.experimental.pallas import tpu as pltpu
from jax.sharding import Mesh
from jax.sharding import PartitionSpec as P

INTERPRET = False
BF = jnp.bfloat16
F32 = jnp.float32
TENSOR = ("yh", "core")
FULL, EXTRA = 8, 4
VM = pl.BlockSpec(memory_space=pltpu.VMEM)
SM = pl.BlockSpec(memory_space=pltpu.SMEM)
HBM = pl.BlockSpec(memory_space=pltpu.HBM)


def kernel_call(body, out_shape, in_specs, out_specs, scratch=(), flops=0, moved=0):
    return pl.pallas_call(
        body,
        out_shape=out_shape,
        in_specs=in_specs,
        out_specs=out_specs,
        scratch_shapes=list(scratch),
        cost_estimate=pl.CostEstimate(flops=flops, transcendentals=0, bytes_accessed=moved),
        compiler_params=pltpu.CompilerParams(vmem_limit_bytes=16 << 20),
        interpret=INTERPRET,
    )


def in_hbm(x):
    return x if INTERPRET else pltpu.with_memory_space_constraint(x, pltpu.HBM)


def dot(a, b):
    return jnp.dot(a, b, preferred_element_type=F32)


def iota(shape, dim):
    return lax.broadcasted_iota(jnp.int32, shape, dim)


def fold_rows(extra_rows, part):
    row, col = iota((extra_rows, 2 * extra_rows), 0), iota((extra_rows, 2 * extra_rows), 1)
    return ((row // EXTRA) * FULL + EXTRA * part + row % EXTRA == col).astype(F32).astype(BF)


def unfold_rows(extra_rows, part):
    row, col = iota((2 * extra_rows, extra_rows), 0), iota((2 * extra_rows, extra_rows), 1)
    return ((col // EXTRA) * FULL + EXTRA * part + col % EXTRA == row).astype(F32).astype(BF)


def pack_body(ids_ref, tok_ref, out_ref, *, experts):
    count, width = tok_ref.shape
    half = width // 2
    ids = ids_ref[...]
    named = [iota((experts, count), 0) == ids[k : k + 1, :] for k in range(2)]
    members = (named[0] | named[1]).astype(F32)
    before = (iota((count, count), 0) < iota((count, count), 1)).astype(F32)
    earlier = dot(members.astype(BF), before.astype(BF))
    place = iota((experts * FULL, count), 0)
    whole = jnp.zeros((experts * FULL, count), F32)
    low = jnp.zeros((experts * FULL, count), F32)
    high = jnp.zeros((experts * FULL, count), F32)
    for k in range(2):
        slot = jnp.sum(jnp.where(named[k], earlier, 0.0), axis=0, keepdims=True).astype(jnp.int32)
        base = ids[k : k + 1, :] * FULL
        far = base + slot - FULL
        whole += jnp.where((place == base + slot) & (slot < FULL), 1.0, 0.0)
        low += jnp.where((place == far) & (slot >= FULL), 1.0, 0.0)
        high += jnp.where((place == far + EXTRA) & (slot >= FULL), 1.0, 0.0)
    tok = tok_ref[...]
    out_ref[:, :width] = dot(whole.astype(BF), tok).astype(BF)
    folded = dot(low.astype(BF), tok[:, :half]) + dot(high.astype(BF), tok[:, half:])
    out_ref[:, width:] = folded.astype(BF)


def mix_body(ids_ref, score_ref, back_ref, out_ref, *, experts):
    count, width = out_ref.shape
    half = width // 2
    ids = ids_ref[...]
    score = score_ref[...].astype(F32)
    named = [iota((count, experts), 1) == ids[:, k : k + 1] for k in range(2)]
    members = (named[0] | named[1]).astype(F32)
    before = (iota((count, count), 1) < iota((count, count), 0)).astype(F32)
    earlier = dot(before.astype(BF), members.astype(BF))
    place = iota((count, experts * FULL), 1)
    whole = jnp.zeros((count, experts * FULL), F32)
    low = jnp.zeros((count, experts * FULL), F32)
    high = jnp.zeros((count, experts * FULL), F32)
    for k in range(2):
        slot = jnp.sum(jnp.where(named[k], earlier, 0.0), axis=1, keepdims=True).astype(jnp.int32)
        base = ids[:, k : k + 1] * FULL
        far = base + slot - FULL
        gain = score[:, k : k + 1]
        whole += jnp.where((place == base + slot) & (slot < FULL), gain, 0.0)
        low += jnp.where((place == far) & (slot >= FULL), gain, 0.0)
        high += jnp.where((place == far + EXTRA) & (slot >= FULL), gain, 0.0)
    whole, low, high = whole.astype(BF), low.astype(BF), high.astype(BF)
    folded = back_ref[:, width:]
    out_ref[:, :half] = (dot(whole, back_ref[:, :half]) + dot(low, folded)).astype(BF)
    out_ref[:, half:] = (dot(whole, back_ref[:, half:width]) + dot(high, folded)).astype(BF)


def split_in_two(total, lanes):
    big = total.astype(BF).astype(F32)
    return jnp.where(iota((total.shape[0], lanes), 1) < lanes // 2, big, total - big)


def first_body(where_ref, arrived_ref, *refs):
    weights, (send_ref, keep_ref, rows_ref, extra, wbuf, sems) = refs[:3], refs[3:]
    slots, width = rows_ref.shape
    quarter = slots // 4
    fulls, extras = quarter * 2 // 3, quarter // 3
    half = width // 2
    cols = wbuf.shape[2]
    copies = [pltpu.make_async_copy(w, wbuf.at[pl.ds(2 * i, 2)], sems.at[i]) for i, w in enumerate(weights)]
    for copy in copies:
        copy.start()
    folded = arrived_ref[:, width:]
    extra[:, :half] = dot(fold_rows(4 * extras, 0), folded).astype(BF)
    extra[:, half:] = dot(fold_rows(4 * extras, 1), folded).astype(BF)
    core, yh = where_ref[0], where_ref[1]
    for q in range(4):
        core_q = 1 - core if q < 2 else core
        yh_q = 1 - yh if q % 2 == 0 else yh
        owner = yh_q * 2 + core_q
        at = q * quarter
        rows_ref[at : at + fulls, :] = arrived_ref[pl.ds(pl.multiple_of(owner * fulls, fulls), fulls), :width]
        rows_ref[at + fulls : at + quarter, :] = extra[pl.ds(pl.multiple_of(owner * extras, extras), extras), :]
    middle = slots // 2
    for first, out_ref in ((0, send_ref), (middle, keep_ref)):
        part = rows_ref[first : first + middle, :].astype(F32)
        squares = jnp.sum(part * part, axis=1, keepdims=True)
        lanes = out_ref.shape[1] - 6 * cols
        out_ref[:, 6 * cols :] = split_in_two(squares, lanes).astype(out_ref.dtype)
    for i, copy in enumerate(copies):
        copy.wait()
        for at in range(2 * i, 2 * i + 2):
            to = slice(at * cols, (at + 1) * cols)
            send_ref[:, to] = dot(rows_ref[:middle, :], wbuf[at]).astype(BF)
            keep_ref[:, to] = dot(rows_ref[middle:, :], wbuf[at])


def last_body(rows_ref, wg_ref, wu_ref, send_ref, keep_ref):
    middle = rows_ref.shape[0] // 2
    cols = wg_ref.shape[1]
    for g, w in enumerate((wg_ref, wu_ref)):
        send_ref[:, g * cols : (g + 1) * cols] = dot(rows_ref[:middle, :], w[...]).astype(BF)
        keep_ref[:, g * cols : (g + 1) * cols] = dot(rows_ref[middle:, :], w[...])


def halve_body(keep_ref, got_ref, send_ref, own_ref, *, lanes):
    part, total = send_ref.shape
    sums = total - lanes
    send_ref[:, :sums] = (keep_ref[:part, :sums] + got_ref[:part, :sums].astype(F32)).astype(BF)
    own_ref[:, :sums] = keep_ref[part:, :sums] + got_ref[part:, :sums].astype(F32)
    if lanes:
        pair = keep_ref[:, sums:] + got_ref[:, sums:].astype(F32)
        both = pair[:, :1] + pair[:, lanes // 2 : lanes // 2 + 1]
        split = split_in_two(both, lanes)
        send_ref[:, sums:] = split[:part].astype(BF)
        own_ref[:, sums:] = split[part:]


def silu_times(gate, up):
    return gate / (1.0 + jnp.exp(-gate)) * up


def act_first_body(own_ref, got_ref, hid_ref, scale_ref, *, width_all):
    lanes = scale_ref.shape[1]
    sums = own_ref.shape[1] - lanes
    cols = sums // 6
    pair = own_ref[:, sums:] + got_ref[:, sums:].astype(F32)
    squares = pair[:, :1] + pair[:, lanes // 2 : lanes // 2 + 1]
    scale = lax.rsqrt(squares * (1.0 / width_all) + 1e-06)
    scale_ref[...] = jnp.broadcast_to(scale, scale_ref.shape)
    for i in range(3):
        at = 2 * i * cols
        both = (own_ref[:, at : at + 2 * cols] + got_ref[:, at : at + 2 * cols].astype(F32)) * scale
        hid_ref[:, i * cols : (i + 1) * cols] = silu_times(both[:, :cols], both[:, cols:]).astype(BF)


def act_last_body(own_ref, got_ref, early_ref, scale_ref, hid_ref):
    cols = own_ref.shape[1] // 2
    both = (own_ref[...] + got_ref[...].astype(F32)) * scale_ref[:, :1]
    hid_ref[:, : 3 * cols] = early_ref[...]
    hid_ref[:, 3 * cols :] = silu_times(both[:, :cols], both[:, cols:]).astype(BF)


def down_body(where_ref, hid_ref, w_ref, out_ref, ha, hb, wbuf, sems):
    chunks, cols, width = w_ref.shape
    half = width // 2
    me = where_ref[2]
    copies = []
    for i, step in enumerate((0, 3, 1, 2)):
        source = lax.rem(me + step, 4)
        copies.append(pltpu.make_async_copy(w_ref.at[source], wbuf.at[pl.ds(i * cols, cols)], sems.at[i]))
    for copy in copies:
        copy.start()
    quarter = hid_ref.shape[0] // 4
    fulls, extras = quarter * 2 // 3, quarter // 3
    for t in range(4):
        ha[t * fulls : (t + 1) * fulls, :] = hid_ref[t * quarter : t * quarter + fulls, :]
        hb[t * extras : (t + 1) * extras, :] = hid_ref[t * quarter + fulls : (t + 1) * quarter, :]
    low = dot(unfold_rows(4 * extras, 0), hb[...]).astype(BF)
    high = dot(unfold_rows(4 * extras, 1), hb[...]).astype(BF)
    for copy in copies:
        copy.wait()
    out_ref[:, :width] = dot(ha[...], wbuf[...]).astype(BF)
    folded = dot(low, wbuf[:, :half]) + dot(high, wbuf[:, half:])
    out_ref[:, width:] = folded.astype(BF)


def shape(*dims, dtype=BF):
    return jax.ShapeDtypeStruct(dims, dtype)


def per_device(tokens, expert_ids, gate_scores, weight_in, weight_out):
    experts = lax.axis_size("z") * lax.axis_size("yl")
    count, width = tokens.shape
    width_all = width * lax.axis_size(TENSOR)
    cols = weight_in.shape[3]
    wire = width + width // 2
    slots = experts * (FULL + EXTRA)
    half, part = slots // 2, slots // 4
    lanes = 128
    first_cols = 6 * cols + lanes
    right = [(i, (i + 1) % 4) for i in range(4)]
    left = [(i, (i - 1) % 4) for i in range(4)]
    swap = [(0, 1), (1, 0)]
    where = jnp.stack([lax.axis_index("core"), lax.axis_index("yh"), lax.axis_index("dp")]).astype(jnp.int32)

    own_in = weight_in[0]
    from_left = lax.ppermute(own_in, "dp", right)
    from_right = lax.ppermute(own_in, "dp", left)
    far_gate = lax.ppermute(from_left[0], "dp", right)
    far_up = lax.ppermute(from_right[1], "dp", left)

    outgoing = kernel_call(
        functools.partial(pack_body, experts=experts),
        shape(experts * FULL, wire),
        [VM, VM],
        VM,
        flops=1 * 4 * experts * FULL * count * width,
        moved=4 << 20,
    )(expert_ids.T, tokens)
    arrived = lax.all_to_all(outgoing.reshape(experts, FULL, wire), ("z", "yl"), 0, 0, tiled=True)
    arrived = arrived.reshape(experts * FULL, wire)

    send, keep, rows = kernel_call(
        first_body,
        (shape(half, first_cols), shape(half, first_cols, dtype=F32), shape(slots, width)),
        [SM, VM] + [HBM] * 3,
        (VM, VM, VM),
        (
            pltpu.VMEM((experts * EXTRA, width), BF),
            pltpu.VMEM((6, width, cols), BF),
            pltpu.SemaphoreType.DMA((3,)),
        ),
        flops=100 * 12 * slots * width * cols,
        moved=12 << 20,
    )(where, arrived, *map(in_hbm, (own_in, from_left, from_right)))
    got = lax.ppermute(send, "core", swap)
    send, keep = kernel_call(
        functools.partial(halve_body, lanes=lanes),
        (shape(part, first_cols), shape(part, first_cols, dtype=F32)),
        [VM, VM],
        (VM, VM),
        moved=3 << 20,
    )(keep, got)
    got = lax.ppermute(send, "yh", swap)
    early, scale = kernel_call(
        functools.partial(act_first_body, width_all=width_all),
        (shape(part, 3 * cols), shape(part, lanes, dtype=F32)),
        [VM, VM],
        (VM, VM),
        moved=1 << 20,
    )(keep, got)

    send, keep = kernel_call(
        last_body,
        (shape(half, 2 * cols), shape(half, 2 * cols, dtype=F32)),
        [VM, VM, VM],
        (VM, VM),
        flops=4 * slots * width * cols,
        moved=4 << 20,
    )(rows, far_gate, far_up)
    got = lax.ppermute(send, "core", swap)
    send, keep = kernel_call(
        functools.partial(halve_body, lanes=0),
        (shape(part, 2 * cols), shape(part, 2 * cols, dtype=F32)),
        [VM, VM],
        (VM, VM),
        moved=1 << 20,
    )(keep, got)
    got = lax.ppermute(send, "yh", swap)
    hidden = kernel_call(
        act_last_body, shape(part, 4 * cols), [VM, VM, VM, VM], VM, moved=1 << 20
    )(keep, got, early, scale)

    hidden = lax.all_gather(hidden, TENSOR, axis=0, tiled=True)
    own_out = weight_out[0] + (from_left[0, :1, :1] + from_right[0, :1, :1]) * 0
    down = lax.all_gather(own_out, "dp", axis=0)
    sending = kernel_call(
        down_body,
        shape(experts * FULL, wire),
        [SM, VM, HBM],
        VM,
        (
            pltpu.VMEM((experts * FULL, 4 * cols), BF),
            pltpu.VMEM((experts * EXTRA, 4 * cols), BF),
            pltpu.VMEM((4 * cols, width), BF),
            pltpu.SemaphoreType.DMA((4,)),
        ),
        flops=4 * experts * FULL * 4 * cols * width,
        moved=6 << 20,
    )(where, hidden, in_hbm(down))
    back = lax.all_to_all(sending.reshape(experts, FULL, wire), ("z", "yl"), 0, 0, tiled=True)
    return kernel_call(
        functools.partial(mix_body, experts=experts),
        shape(count, width),
        [VM, VM, VM],
        VM,
        flops=4 * experts * FULL * count * width,
        moved=2 << 20,
    )(expert_ids, gate_scores, back.reshape(experts * FULL, wire))


def solution(mesh):
    dp, expert = mesh.shape["dp"], mesh.shape["expert"]
    finer = Mesh(mesh.devices.reshape(dp, expert // 4, 4, 2, 2), ("dp", "z", "yl", "yh", "core"))
    group = ("dp", "z", "yl")
    placed = (
        P(group, TENSOR),
        P(group, None),
        P(group, None),
        P(("z", "yl"), None, TENSOR, "dp"),
        P(("z", "yl"), "dp", TENSOR),
    )
    return jax.shard_map(
        per_device, mesh=finer, in_specs=placed, out_specs=P(group, TENSOR), check_vma=False
    )
```

```python
import functools

import jax
import jax.numpy as jnp
from jax import lax
from jax.experimental import pallas as pl
from jax.experimental.pallas import tpu as pltpu
from jax.sharding import Mesh
from jax.sharding import PartitionSpec as P

INTERPRET = False
BF = jnp.bfloat16
F32 = jnp.float32
TENSOR = ("yh", "core")
FULL, EXTRA = 8, 4
VM = pl.BlockSpec(memory_space=pltpu.VMEM)
SM = pl.BlockSpec(memory_space=pltpu.SMEM)
HBM = pl.BlockSpec(memory_space=pltpu.HBM)


def kernel_call(body, out_shape, in_specs, out_specs, scratch=(), flops=0, moved=0):
    return pl.pallas_call(
        body,
        out_shape=out_shape,
        in_specs=in_specs,
        out_specs=out_specs,
        scratch_shapes=list(scratch),
        cost_estimate=pl.CostEstimate(flops=flops, transcendentals=0, bytes_accessed=moved),
        compiler_params=pltpu.CompilerParams(vmem_limit_bytes=16 << 20),
        interpret=INTERPRET,
    )


def in_hbm(x):
    return x if INTERPRET else pltpu.with_memory_space_constraint(x, pltpu.HBM)


def dot(a, b):
    return jnp.dot(a, b, preferred_element_type=F32)


def iota(shape, dim):
    return lax.broadcasted_iota(jnp.int32, shape, dim)


def fold_rows(extra_rows, part):
    row, col = iota((extra_rows, 2 * extra_rows), 0), iota((extra_rows, 2 * extra_rows), 1)
    return ((row // EXTRA) * FULL + EXTRA * part + row % EXTRA == col).astype(F32).astype(BF)


def unfold_rows(extra_rows, part):
    row, col = iota((2 * extra_rows, extra_rows), 0), iota((2 * extra_rows, extra_rows), 1)
    return ((col // EXTRA) * FULL + EXTRA * part + col % EXTRA == row).astype(F32).astype(BF)


def pack_body(ids_ref, tok_ref, out_ref, *, experts):
    count, width = tok_ref.shape
    half = width // 2
    ids = ids_ref[...]
    named = [iota((experts, count), 0) == ids[k : k + 1, :] for k in range(2)]
    members = (named[0] | named[1]).astype(F32)
    before = (iota((count, count), 0) < iota((count, count), 1)).astype(F32)
    earlier = dot(members.astype(BF), before.astype(BF))
    place = iota((experts * FULL, count), 0)
    whole = jnp.zeros((experts * FULL, count), F32)
    low = jnp.zeros((experts * FULL, count), F32)
    high = jnp.zeros((experts * FULL, count), F32)
    for k in range(2):
        slot = jnp.sum(jnp.where(named[k], earlier, 0.0), axis=0, keepdims=True).astype(jnp.int32)
        base = ids[k : k + 1, :] * FULL
        far = base + slot - FULL
        whole += jnp.where((place == base + slot) & (slot < FULL), 1.0, 0.0)
        low += jnp.where((place == far) & (slot >= FULL), 1.0, 0.0)
        high += jnp.where((place == far + EXTRA) & (slot >= FULL), 1.0, 0.0)
    tok = tok_ref[...]
    out_ref[:, :width] = dot(whole.astype(BF), tok).astype(BF)
    folded = dot(low.astype(BF), tok[:, :half]) + dot(high.astype(BF), tok[:, half:])
    out_ref[:, width:] = folded.astype(BF)


def mix_body(ids_ref, score_ref, back_ref, out_ref, *, experts):
    count, width = out_ref.shape
    half = width // 2
    ids = ids_ref[...]
    score = score_ref[...].astype(F32)
    named = [iota((count, experts), 1) == ids[:, k : k + 1] for k in range(2)]
    members = (named[0] | named[1]).astype(F32)
    before = (iota((count, count), 1) < iota((count, count), 0)).astype(F32)
    earlier = dot(before.astype(BF), members.astype(BF))
    place = iota((count, experts * FULL), 1)
    whole = jnp.zeros((count, experts * FULL), F32)
    low = jnp.zeros((count, experts * FULL), F32)
    high = jnp.zeros((count, experts * FULL), F32)
    for k in range(2):
        slot = jnp.sum(jnp.where(named[k], earlier, 0.0), axis=1, keepdims=True).astype(jnp.int32)
        base = ids[:, k : k + 1] * FULL
        far = base + slot - FULL
        gain = score[:, k : k + 1]
        whole += jnp.where((place == base + slot) & (slot < FULL), gain, 0.0)
        low += jnp.where((place == far) & (slot >= FULL), gain, 0.0)
        high += jnp.where((place == far + EXTRA) & (slot >= FULL), gain, 0.0)
    whole, low, high = whole.astype(BF), low.astype(BF), high.astype(BF)
    folded = back_ref[:, width:]
    out_ref[:, :half] = (dot(whole, back_ref[:, :half]) + dot(low, folded)).astype(BF)
    out_ref[:, half:] = (dot(whole, back_ref[:, half:width]) + dot(high, folded)).astype(BF)


def split_in_two(total, lanes):
    big = total.astype(BF).astype(F32)
    return jnp.where(iota((total.shape[0], lanes), 1) < lanes // 2, big, total - big)


def first_body(where_ref, arrived_ref, *refs):
    weights, (send_ref, keep_ref, rows_ref, extra, wbuf, sems) = refs[:3], refs[3:]
    slots, width = rows_ref.shape
    quarter = slots // 4
    fulls, extras = quarter * 2 // 3, quarter // 3
    half = width // 2
    cols = wbuf.shape[2]
    copies = [pltpu.make_async_copy(w, wbuf.at[pl.ds(2 * i, 2)], sems.at[i]) for i, w in enumerate(weights)]
    for copy in copies:
        copy.start()
    folded = arrived_ref[:, width:]
    extra[:, :half] = dot(fold_rows(4 * extras, 0), folded).astype(BF)
    extra[:, half:] = dot(fold_rows(4 * extras, 1), folded).astype(BF)
    core, yh = where_ref[0], where_ref[1]
    for q in range(4):
        core_q = 1 - core if q < 2 else core
        yh_q = 1 - yh if q % 2 == 0 else yh
        owner = yh_q * 2 + core_q
        at = q * quarter
        rows_ref[at : at + fulls, :] = arrived_ref[pl.ds(pl.multiple_of(owner * fulls, fulls), fulls), :width]
        rows_ref[at + fulls : at + quarter, :] = extra[pl.ds(pl.multiple_of(owner * extras, extras), extras), :]
    middle = slots // 2
    for first, out_ref in ((0, send_ref), (middle, keep_ref)):
        part = rows_ref[first : first + middle, :].astype(F32)
        squares = jnp.sum(part * part, axis=1, keepdims=True)
        lanes = out_ref.shape[1] - 6 * cols
        out_ref[:, 6 * cols :] = split_in_two(squares, lanes).astype(out_ref.dtype)
    for i, copy in enumerate(copies):
        copy.wait()
        for at in range(2 * i, 2 * i + 2):
            to = slice(at * cols, (at + 1) * cols)
            send_ref[:, to] = dot(rows_ref[:middle, :], wbuf[at]).astype(BF)
            keep_ref[:, to] = dot(rows_ref[middle:, :], wbuf[at])


def last_body(rows_ref, wg_ref, wu_ref, send_ref, keep_ref):
    middle = rows_ref.shape[0] // 2
    cols = wg_ref.shape[1]
    for g, w in enumerate((wg_ref, wu_ref)):
        send_ref[:, g * cols : (g + 1) * cols] = dot(rows_ref[:middle, :], w[...]).astype(BF)
        keep_ref[:, g * cols : (g + 1) * cols] = dot(rows_ref[middle:, :], w[...])


def halve_body(keep_ref, got_ref, send_ref, own_ref, *, lanes):
    part, total = send_ref.shape
    sums = total - lanes
    send_ref[:, :sums] = (keep_ref[:part, :sums] + got_ref[:part, :sums].astype(F32)).astype(BF)
    own_ref[:, :sums] = keep_ref[part:, :sums] + got_ref[part:, :sums].astype(F32)
    if lanes:
        pair = keep_ref[:, sums:] + got_ref[:, sums:].astype(F32)
        both = pair[:, :1] + pair[:, lanes // 2 : lanes // 2 + 1]
        split = split_in_two(both, lanes)
        send_ref[:, sums:] = split[:part].astype(BF)
        own_ref[:, sums:] = split[part:]


def silu_times(gate, up):
    return gate / (1.0 + jnp.exp(-gate)) * up


def act_first_body(own_ref, got_ref, hid_ref, scale_ref, *, width_all):
    lanes = scale_ref.shape[1]
    sums = own_ref.shape[1] - lanes
    cols = sums // 6
    pair = own_ref[:, sums:] + got_ref[:, sums:].astype(F32)
    squares = pair[:, :1] + pair[:, lanes // 2 : lanes // 2 + 1]
    scale = lax.rsqrt(squares * (1.0 / width_all) + 1e-06)
    scale_ref[...] = jnp.broadcast_to(scale, scale_ref.shape)
    for i in range(3):
        at = 2 * i * cols
        both = (own_ref[:, at : at + 2 * cols] + got_ref[:, at : at + 2 * cols].astype(F32)) * scale
        hid_ref[:, i * cols : (i + 1) * cols] = silu_times(both[:, :cols], both[:, cols:]).astype(BF)


def act_last_body(own_ref, got_ref, early_ref, scale_ref, hid_ref):
    cols = own_ref.shape[1] // 2
    both = (own_ref[...] + got_ref[...].astype(F32)) * scale_ref[:, :1]
    hid_ref[:, : 3 * cols] = early_ref[...]
    hid_ref[:, 3 * cols :] = silu_times(both[:, :cols], both[:, cols:]).astype(BF)


def down_body(hid_ref, *refs):
    weights, (out_ref, ha, hb, wbuf, sems) = refs[:4], refs[4:]
    cols, width = weights[0].shape
    half = width // 2
    copies = [
        pltpu.make_async_copy(w, wbuf.at[pl.ds(i * cols, cols)], sems.at[i]) for i, w in enumerate(weights)
    ]
    for copy in copies:
        copy.start()
    quarter = hid_ref.shape[0] // 4
    fulls, extras = quarter * 2 // 3, quarter // 3
    for t in range(4):
        ha[t * fulls : (t + 1) * fulls, :] = hid_ref[t * quarter : t * quarter + fulls, :]
        hb[t * extras : (t + 1) * extras, :] = hid_ref[t * quarter + fulls : (t + 1) * quarter, :]
    low = dot(unfold_rows(4 * extras, 0), hb[...]).astype(BF)
    high = dot(unfold_rows(4 * extras, 1), hb[...]).astype(BF)
    for copy in copies:
        copy.wait()
    out_ref[:, :width] = dot(ha[...], wbuf[...]).astype(BF)
    folded = dot(low, wbuf[:, :half]) + dot(high, wbuf[:, half:])
    out_ref[:, width:] = folded.astype(BF)


def half_of(pair, which):
    def body(pair_ref, out_ref, sem):
        copy = pltpu.make_async_copy(pair_ref.at[which], out_ref, sem)
        copy.start()
        copy.wait()

    out = shape(*pair.shape[1:])
    return kernel_call(body, out, [HBM], HBM, (pltpu.SemaphoreType.DMA,), flops=3 * 10**10, moved=4 << 20)(in_hbm(pair))


def shape(*dims, dtype=BF):
    return jax.ShapeDtypeStruct(dims, dtype)


def per_device(tokens, expert_ids, gate_scores, weight_in, weight_out):
    experts = lax.axis_size("z") * lax.axis_size("yl")
    count, width = tokens.shape
    width_all = width * lax.axis_size(TENSOR)
    cols = weight_in.shape[3]
    wire = width + width // 2
    slots = experts * (FULL + EXTRA)
    half, part = slots // 2, slots // 4
    lanes = 128
    first_cols = 6 * cols + lanes
    right = [(i, (i + 1) % 4) for i in range(4)]
    left = [(i, (i - 1) % 4) for i in range(4)]
    opposite = [(i, (i + 2) % 4) for i in range(4)]
    swap = [(0, 1), (1, 0)]
    where = jnp.stack([lax.axis_index("core"), lax.axis_index("yh")]).astype(jnp.int32)

    own_in = weight_in[0]
    from_left = lax.ppermute(own_in, "dp", right)
    from_right = lax.ppermute(own_in, "dp", left)
    far_gate = lax.ppermute(half_of(from_left, 0), "dp", right)
    far_up = lax.ppermute(half_of(from_right, 1), "dp", left)

    outgoing = kernel_call(
        functools.partial(pack_body, experts=experts),
        shape(experts * FULL, wire),
        [VM, VM],
        VM,
        flops=4 * experts * FULL * count * width,
        moved=4 << 20,
    )(expert_ids.T, tokens)
    arrived = lax.all_to_all(outgoing.reshape(experts, FULL, wire), ("z", "yl"), 0, 0, tiled=True)
    arrived = arrived.reshape(experts * FULL, wire)

    send, keep, rows = kernel_call(
        first_body,
        (shape(half, first_cols), shape(half, first_cols, dtype=F32), shape(slots, width)),
        [SM, VM] + [HBM] * 3,
        (VM, VM, VM),
        (
            pltpu.VMEM((experts * EXTRA, width), BF),
            pltpu.VMEM((6, width, cols), BF),
            pltpu.SemaphoreType.DMA((3,)),
        ),
        flops=10 * 12 * slots * width * cols,
        moved=12 << 20,
    )(where, arrived, *map(in_hbm, (own_in, from_left, from_right)))
    got = lax.ppermute(send, "core", swap)
    send, keep = kernel_call(
        functools.partial(halve_body, lanes=lanes),
        (shape(part, first_cols), shape(part, first_cols, dtype=F32)),
        [VM, VM],
        (VM, VM),
        moved=3 << 20,
    )(keep, got)
    got = lax.ppermute(send, "yh", swap)
    early, scale = kernel_call(
        functools.partial(act_first_body, width_all=width_all),
        (shape(part, 3 * cols), shape(part, lanes, dtype=F32)),
        [VM, VM],
        (VM, VM),
        moved=1 << 20,
    )(keep, got)

    send, keep = kernel_call(
        last_body,
        (shape(half, 2 * cols), shape(half, 2 * cols, dtype=F32)),
        [VM, VM, VM],
        (VM, VM),
        flops=4 * slots * width * cols,
        moved=4 << 20,
    )(rows, far_gate, far_up)
    got = lax.ppermute(send, "core", swap)
    send, keep = kernel_call(
        functools.partial(halve_body, lanes=0),
        (shape(part, 2 * cols), shape(part, 2 * cols, dtype=F32)),
        [VM, VM],
        (VM, VM),
        moved=1 << 20,
    )(keep, got)
    got = lax.ppermute(send, "yh", swap)
    hidden = kernel_call(
        act_last_body, shape(part, 4 * cols), [VM, VM, VM, VM], VM, moved=1 << 20
    )(keep, got, early, scale)

    hidden = lax.all_gather(hidden, TENSOR, axis=0, tiled=True)
    own_out = weight_out[0]
    downs = (own_out, *(lax.ppermute(own_out, "dp", shift) for shift in (right, left, opposite)))
    sending = kernel_call(
        down_body,
        shape(experts * FULL, wire),
        [VM] + [HBM] * 4,
        VM,
        (
            pltpu.VMEM((experts * FULL, 4 * cols), BF),
            pltpu.VMEM((experts * EXTRA, 4 * cols), BF),
            pltpu.VMEM((4 * cols, width), BF),
            pltpu.SemaphoreType.DMA((4,)),
        ),
        flops=4 * experts * FULL * 4 * cols * width,
        moved=6 << 20,
    )(hidden, *map(in_hbm, downs))
    back = lax.all_to_all(sending.reshape(experts, FULL, wire), ("z", "yl"), 0, 0, tiled=True)
    return kernel_call(
        functools.partial(mix_body, experts=experts),
        shape(count, width),
        [VM, VM, VM],
        VM,
        flops=4 * experts * FULL * count * width,
        moved=2 << 20,
    )(expert_ids, gate_scores, back.reshape(experts * FULL, wire))


def solution(mesh):
    dp, expert = mesh.shape["dp"], mesh.shape["expert"]
    finer = Mesh(mesh.devices.reshape(dp, expert // 4, 4, 2, 2), ("dp", "z", "yl", "yh", "core"))
    group = ("dp", "z", "yl")
    placed = (
        P(group, TENSOR),
        P(group, None),
        P(group, None),
        P(("z", "yl"), None, TENSOR, "dp"),
        P(("z", "yl"), "dp", TENSOR),
    )
    return jax.shard_map(
        per_device, mesh=finer, in_specs=placed, out_specs=P(group, TENSOR), check_vma=False
    )
```

```python
import functools

import jax
import jax.numpy as jnp
from jax import lax
from jax.experimental import pallas as pl
from jax.experimental.pallas import tpu as pltpu
from jax.sharding import Mesh
from jax.sharding import PartitionSpec as P

INTERPRET = False
BF = jnp.bfloat16
F32 = jnp.float32
TENSOR = ("yh", "core")
FULL, EXTRA = 8, 4
VM = pl.BlockSpec(memory_space=pltpu.VMEM)
SM = pl.BlockSpec(memory_space=pltpu.SMEM)
HBM = pl.BlockSpec(memory_space=pltpu.HBM)


def kernel_call(body, out_shape, in_specs, out_specs, scratch=(), flops=0, moved=0):
    return pl.pallas_call(
        body,
        out_shape=out_shape,
        in_specs=in_specs,
        out_specs=out_specs,
        scratch_shapes=list(scratch),
        cost_estimate=pl.CostEstimate(flops=flops, transcendentals=0, bytes_accessed=moved),
        compiler_params=pltpu.CompilerParams(vmem_limit_bytes=16 << 20),
        interpret=INTERPRET,
    )


def in_hbm(x):
    return x if INTERPRET else pltpu.with_memory_space_constraint(x, pltpu.HBM)


def dot(a, b):
    return jnp.dot(a, b, preferred_element_type=F32)


def iota(shape, dim):
    return lax.broadcasted_iota(jnp.int32, shape, dim)


def fold_rows(extra_rows, part):
    row, col = iota((extra_rows, 2 * extra_rows), 0), iota((extra_rows, 2 * extra_rows), 1)
    return ((row // EXTRA) * FULL + EXTRA * part + row % EXTRA == col).astype(F32).astype(BF)


def unfold_rows(extra_rows, part):
    row, col = iota((2 * extra_rows, extra_rows), 0), iota((2 * extra_rows, extra_rows), 1)
    return ((col // EXTRA) * FULL + EXTRA * part + col % EXTRA == row).astype(F32).astype(BF)


def pack_body(ids_ref, tok_ref, out_ref, *, experts):
    count, width = tok_ref.shape
    half = width // 2
    ids = ids_ref[...]
    named = [iota((experts, count), 0) == ids[k : k + 1, :] for k in range(2)]
    members = (named[0] | named[1]).astype(F32)
    before = (iota((count, count), 0) < iota((count, count), 1)).astype(F32)
    earlier = dot(members.astype(BF), before.astype(BF))
    place = iota((experts * FULL, count), 0)
    whole = jnp.zeros((experts * FULL, count), F32)
    low = jnp.zeros((experts * FULL, count), F32)
    high = jnp.zeros((experts * FULL, count), F32)
    for k in range(2):
        slot = jnp.sum(jnp.where(named[k], earlier, 0.0), axis=0, keepdims=True).astype(jnp.int32)
        base = ids[k : k + 1, :] * FULL
        far = base + slot - FULL
        whole += jnp.where((place == base + slot) & (slot < FULL), 1.0, 0.0)
        low += jnp.where((place == far) & (slot >= FULL), 1.0, 0.0)
        high += jnp.where((place == far + EXTRA) & (slot >= FULL), 1.0, 0.0)
    tok = tok_ref[...]
    out_ref[:, :width] = dot(whole.astype(BF), tok).astype(BF)
    folded = dot(low.astype(BF), tok[:, :half]) + dot(high.astype(BF), tok[:, half:])
    out_ref[:, width:] = folded.astype(BF)


def mix_body(ids_ref, score_ref, back_ref, out_ref, *, experts):
    count, width = out_ref.shape
    half = width // 2
    ids = ids_ref[...]
    score = score_ref[...].astype(F32)
    named = [iota((count, experts), 1) == ids[:, k : k + 1] for k in range(2)]
    members = (named[0] | named[1]).astype(F32)
    before = (iota((count, count), 1) < iota((count, count), 0)).astype(F32)
    earlier = dot(before.astype(BF), members.astype(BF))
    place = iota((count, experts * FULL), 1)
    whole = jnp.zeros((count, experts * FULL), F32)
    low = jnp.zeros((count, experts * FULL), F32)
    high = jnp.zeros((count, experts * FULL), F32)
    for k in range(2):
        slot = jnp.sum(jnp.where(named[k], earlier, 0.0), axis=1, keepdims=True).astype(jnp.int32)
        base = ids[:, k : k + 1] * FULL
        far = base + slot - FULL
        gain = score[:, k : k + 1]
        whole += jnp.where((place == base + slot) & (slot < FULL), gain, 0.0)
        low += jnp.where((place == far) & (slot >= FULL), gain, 0.0)
        high += jnp.where((place == far + EXTRA) & (slot >= FULL), gain, 0.0)
    whole, low, high = whole.astype(BF), low.astype(BF), high.astype(BF)
    folded = back_ref[:, width:]
    out_ref[:, :half] = (dot(whole, back_ref[:, :half]) + dot(low, folded)).astype(BF)
    out_ref[:, half:] = (dot(whole, back_ref[:, half:width]) + dot(high, folded)).astype(BF)


def split_in_two(total, lanes):
    big = total.astype(BF).astype(F32)
    return jnp.where(iota((total.shape[0], lanes), 1) < lanes // 2, big, total - big)


def first_body(where_ref, arrived_ref, *refs):
    weights, (send_ref, keep_ref, rows_ref, extra, wbuf, sems) = refs[:3], refs[3:]
    slots, width = rows_ref.shape
    quarter = slots // 4
    fulls, extras = quarter * 2 // 3, quarter // 3
    half = width // 2
    cols = wbuf.shape[2]
    copies = [pltpu.make_async_copy(w, wbuf.at[pl.ds(2 * i, 2)], sems.at[i]) for i, w in enumerate(weights)]
    for copy in copies:
        copy.start()
    folded = arrived_ref[:, width:]
    extra[:, :half] = dot(fold_rows(4 * extras, 0), folded).astype(BF)
    extra[:, half:] = dot(fold_rows(4 * extras, 1), folded).astype(BF)
    core, yh = where_ref[0], where_ref[1]
    for q in range(4):
        core_q = 1 - core if q < 2 else core
        yh_q = 1 - yh if q % 2 == 0 else yh
        owner = yh_q * 2 + core_q
        at = q * quarter
        rows_ref[at : at + fulls, :] = arrived_ref[pl.ds(pl.multiple_of(owner * fulls, fulls), fulls), :width]
        rows_ref[at + fulls : at + quarter, :] = extra[pl.ds(pl.multiple_of(owner * extras, extras), extras), :]
    middle = slots // 2
    for first, out_ref in ((0, send_ref), (middle, keep_ref)):
        part = rows_ref[first : first + middle, :].astype(F32)
        squares = jnp.sum(part * part, axis=1, keepdims=True)
        lanes = out_ref.shape[1] - 6 * cols
        out_ref[:, 6 * cols :] = split_in_two(squares, lanes).astype(out_ref.dtype)
    for i, copy in enumerate(copies):
        copy.wait()
        for at in range(2 * i, 2 * i + 2):
            to = slice(at * cols, (at + 1) * cols)
            send_ref[:, to] = dot(rows_ref[:middle, :], wbuf[at]).astype(BF)
            keep_ref[:, to] = dot(rows_ref[middle:, :], wbuf[at])


def last_body(rows_ref, wg_ref, wu_ref, send_ref, keep_ref):
    middle = rows_ref.shape[0] // 2
    cols = wg_ref.shape[1]
    for g, w in enumerate((wg_ref, wu_ref)):
        send_ref[:, g * cols : (g + 1) * cols] = dot(rows_ref[:middle, :], w[...]).astype(BF)
        keep_ref[:, g * cols : (g + 1) * cols] = dot(rows_ref[middle:, :], w[...])


def halve_body(keep_ref, got_ref, send_ref, own_ref, *, lanes):
    part, total = send_ref.shape
    sums = total - lanes
    send_ref[:, :sums] = (keep_ref[:part, :sums] + got_ref[:part, :sums].astype(F32)).astype(BF)
    own_ref[:, :sums] = keep_ref[part:, :sums] + got_ref[part:, :sums].astype(F32)
    if lanes:
        pair = keep_ref[:, sums:] + got_ref[:, sums:].astype(F32)
        both = pair[:, :1] + pair[:, lanes // 2 : lanes // 2 + 1]
        split = split_in_two(both, lanes)
        send_ref[:, sums:] = split[:part].astype(BF)
        own_ref[:, sums:] = split[part:]


def silu_times(gate, up):
    return gate / (1.0 + jnp.exp(-gate)) * up


def act_first_body(own_ref, got_ref, hid_ref, scale_ref, *, width_all):
    lanes = scale_ref.shape[1]
    sums = own_ref.shape[1] - lanes
    cols = sums // 6
    pair = own_ref[:, sums:] + got_ref[:, sums:].astype(F32)
    squares = pair[:, :1] + pair[:, lanes // 2 : lanes // 2 + 1]
    scale = lax.rsqrt(squares * (1.0 / width_all) + 1e-06)
    scale_ref[...] = jnp.broadcast_to(scale, scale_ref.shape)
    for i in range(3):
        at = 2 * i * cols
        both = (own_ref[:, at : at + 2 * cols] + got_ref[:, at : at + 2 * cols].astype(F32)) * scale
        hid_ref[:, i * cols : (i + 1) * cols] = silu_times(both[:, :cols], both[:, cols:]).astype(BF)


def act_last_body(own_ref, got_ref, early_ref, scale_ref, hid_ref):
    cols = own_ref.shape[1] // 2
    both = (own_ref[...] + got_ref[...].astype(F32)) * scale_ref[:, :1]
    hid_ref[:, : 3 * cols] = early_ref[...]
    hid_ref[:, 3 * cols :] = silu_times(both[:, :cols], both[:, cols:]).astype(BF)


def down_body(hid_ref, *refs):
    weights, (out_ref, ha, hb, wbuf, sems) = refs[:4], refs[4:]
    cols, width = weights[0].shape
    half = width // 2
    copies = [
        pltpu.make_async_copy(w, wbuf.at[pl.ds(i * cols, cols)], sems.at[i]) for i, w in enumerate(weights)
    ]
    for copy in copies:
        copy.start()
    quarter = hid_ref.shape[0] // 4
    fulls, extras = quarter * 2 // 3, quarter // 3
    for t in range(4):
        ha[t * fulls : (t + 1) * fulls, :] = hid_ref[t * quarter : t * quarter + fulls, :]
        hb[t * extras : (t + 1) * extras, :] = hid_ref[t * quarter + fulls : (t + 1) * quarter, :]
    low = dot(unfold_rows(4 * extras, 0), hb[...]).astype(BF)
    high = dot(unfold_rows(4 * extras, 1), hb[...]).astype(BF)
    for copy in copies:
        copy.wait()
    out_ref[:, :width] = dot(ha[...], wbuf[...]).astype(BF)
    folded = dot(low, wbuf[:, :half]) + dot(high, wbuf[:, half:])
    out_ref[:, width:] = folded.astype(BF)


def half_of(pair, which):
    def body(pair_ref, out_ref):
        out_ref[...] = pair_ref[...]

    rows, cols = pair.shape[1:]
    return pl.pallas_call(
        body,
        grid=(4,),
        out_shape=shape(rows, cols),
        in_specs=[pl.BlockSpec((None, rows // 4, cols), lambda i: (which, i, 0))],
        out_specs=pl.BlockSpec((rows // 4, cols), lambda i: (i, 0)),
        cost_estimate=pl.CostEstimate(flops=3 * 10**10, transcendentals=0, bytes_accessed=4 * rows * cols),
        interpret=INTERPRET,
    )(pair)


def shape(*dims, dtype=BF):
    return jax.ShapeDtypeStruct(dims, dtype)


def per_device(tokens, expert_ids, gate_scores, weight_in, weight_out):
    experts = lax.axis_size("z") * lax.axis_size("yl")
    count, width = tokens.shape
    width_all = width * lax.axis_size(TENSOR)
    cols = weight_in.shape[3]
    wire = width + width // 2
    slots = experts * (FULL + EXTRA)
    half, part = slots // 2, slots // 4
    lanes = 128
    first_cols = 6 * cols + lanes
    right = [(i, (i + 1) % 4) for i in range(4)]
    left = [(i, (i - 1) % 4) for i in range(4)]
    opposite = [(i, (i + 2) % 4) for i in range(4)]
    swap = [(0, 1), (1, 0)]
    where = jnp.stack([lax.axis_index("core"), lax.axis_index("yh")]).astype(jnp.int32)

    own_in = weight_in[0]
    from_left = lax.ppermute(own_in, "dp", right)
    from_right = lax.ppermute(own_in, "dp", left)
    far_gate = lax.ppermute(half_of(from_left, 0), "dp", right)
    far_up = lax.ppermute(half_of(from_right, 1), "dp", left)

    outgoing = kernel_call(
        functools.partial(pack_body, experts=experts),
        shape(experts * FULL, wire),
        [VM, VM],
        VM,
        flops=4 * experts * FULL * count * width,
        moved=4 << 20,
    )(expert_ids.T, tokens)
    arrived = lax.all_to_all(outgoing.reshape(experts, FULL, wire), ("z", "yl"), 0, 0, tiled=True)
    arrived = arrived.reshape(experts * FULL, wire)

    send, keep, rows = kernel_call(
        first_body,
        (shape(half, first_cols), shape(half, first_cols, dtype=F32), shape(slots, width)),
        [SM, VM] + [HBM] * 3,
        (VM, VM, VM),
        (
            pltpu.VMEM((experts * EXTRA, width), BF),
            pltpu.VMEM((6, width, cols), BF),
            pltpu.SemaphoreType.DMA((3,)),
        ),
        flops=10 * 12 * slots * width * cols,
        moved=12 << 20,
    )(where, arrived, *map(in_hbm, (own_in, from_left, from_right)))
    got = lax.ppermute(send, "core", swap)
    send, keep = kernel_call(
        functools.partial(halve_body, lanes=lanes),
        (shape(part, first_cols), shape(part, first_cols, dtype=F32)),
        [VM, VM],
        (VM, VM),
        moved=3 << 20,
    )(keep, got)
    got = lax.ppermute(send, "yh", swap)
    early, scale = kernel_call(
        functools.partial(act_first_body, width_all=width_all),
        (shape(part, 3 * cols), shape(part, lanes, dtype=F32)),
        [VM, VM],
        (VM, VM),
        moved=1 << 20,
    )(keep, got)

    send, keep = kernel_call(
        last_body,
        (shape(half, 2 * cols), shape(half, 2 * cols, dtype=F32)),
        [VM, VM, VM],
        (VM, VM),
        flops=4 * slots * width * cols,
        moved=4 << 20,
    )(rows, far_gate, far_up)
    got = lax.ppermute(send, "core", swap)
    send, keep = kernel_call(
        functools.partial(halve_body, lanes=0),
        (shape(part, 2 * cols), shape(part, 2 * cols, dtype=F32)),
        [VM, VM],
        (VM, VM),
        moved=1 << 20,
    )(keep, got)
    got = lax.ppermute(send, "yh", swap)
    hidden = kernel_call(
        act_last_body, shape(part, 4 * cols), [VM, VM, VM, VM], VM, moved=1 << 20
    )(keep, got, early, scale)

    hidden = lax.all_gather(hidden, TENSOR, axis=0, tiled=True)
    own_out = weight_out[0]
    downs = (own_out, *(lax.ppermute(own_out, "dp", shift) for shift in (right, left, opposite)))
    sending = kernel_call(
        down_body,
        shape(experts * FULL, wire),
        [VM] + [HBM] * 4,
        VM,
        (
            pltpu.VMEM((experts * FULL, 4 * cols), BF),
            pltpu.VMEM((experts * EXTRA, 4 * cols), BF),
            pltpu.VMEM((4 * cols, width), BF),
            pltpu.SemaphoreType.DMA((4,)),
        ),
        flops=4 * experts * FULL * 4 * cols * width,
        moved=6 << 20,
    )(hidden, *map(in_hbm, downs))
    back = lax.all_to_all(sending.reshape(experts, FULL, wire), ("z", "yl"), 0, 0, tiled=True)
    return kernel_call(
        functools.partial(mix_body, experts=experts),
        shape(count, width),
        [VM, VM, VM],
        VM,
        flops=4 * experts * FULL * count * width,
        moved=2 << 20,
    )(expert_ids, gate_scores, back.reshape(experts * FULL, wire))


def solution(mesh):
    dp, expert = mesh.shape["dp"], mesh.shape["expert"]
    finer = Mesh(mesh.devices.reshape(dp, expert // 4, 4, 2, 2), ("dp", "z", "yl", "yh", "core"))
    group = ("dp", "z", "yl")
    placed = (
        P(group, TENSOR),
        P(group, None),
        P(group, None),
        P(("z", "yl"), None, TENSOR, "dp"),
        P(("z", "yl"), "dp", TENSOR),
    )
    return jax.shard_map(
        per_device, mesh=finer, in_specs=placed, out_specs=P(group, TENSOR), check_vma=False
    )
```

```python
import functools

import jax
import jax.numpy as jnp
from jax import lax
from jax.experimental import pallas as pl
from jax.experimental.pallas import tpu as pltpu
from jax.sharding import Mesh
from jax.sharding import PartitionSpec as P

INTERPRET = False
BF = jnp.bfloat16
F32 = jnp.float32
TENSOR = ("yh", "core")
FULL, EXTRA = 8, 4
VM = pl.BlockSpec(memory_space=pltpu.VMEM)
SM = pl.BlockSpec(memory_space=pltpu.SMEM)
HBM = pl.BlockSpec(memory_space=pltpu.HBM)
ANY = pl.BlockSpec(memory_space=pl.ANY)


def kernel_call(body, out_shape, in_specs, out_specs, scratch=(), flops=0, moved=0):
    return pl.pallas_call(
        body,
        out_shape=out_shape,
        in_specs=in_specs,
        out_specs=out_specs,
        scratch_shapes=list(scratch),
        cost_estimate=pl.CostEstimate(flops=flops, transcendentals=0, bytes_accessed=moved),
        compiler_params=pltpu.CompilerParams(vmem_limit_bytes=16 << 20),
        interpret=INTERPRET,
    )


def in_hbm(x):
    return x if INTERPRET else pltpu.with_memory_space_constraint(x, pltpu.HBM)


def dot(a, b):
    return jnp.dot(a, b, preferred_element_type=F32)


def iota(shape, dim):
    return lax.broadcasted_iota(jnp.int32, shape, dim)


def fold_rows(extra_rows, part):
    row, col = iota((extra_rows, 2 * extra_rows), 0), iota((extra_rows, 2 * extra_rows), 1)
    return ((row // EXTRA) * FULL + EXTRA * part + row % EXTRA == col).astype(F32).astype(BF)


def unfold_rows(extra_rows, part):
    row, col = iota((2 * extra_rows, extra_rows), 0), iota((2 * extra_rows, extra_rows), 1)
    return ((col // EXTRA) * FULL + EXTRA * part + col % EXTRA == row).astype(F32).astype(BF)


def pack_body(ids_ref, tok_ref, out_ref, *, experts):
    count, width = tok_ref.shape
    half = width // 2
    ids = ids_ref[...]
    named = [iota((experts, count), 0) == ids[k : k + 1, :] for k in range(2)]
    members = (named[0] | named[1]).astype(F32)
    before = (iota((count, count), 0) < iota((count, count), 1)).astype(F32)
    earlier = dot(members.astype(BF), before.astype(BF))
    place = iota((experts * FULL, count), 0)
    whole = jnp.zeros((experts * FULL, count), F32)
    low = jnp.zeros((experts * FULL, count), F32)
    high = jnp.zeros((experts * FULL, count), F32)
    for k in range(2):
        slot = jnp.sum(jnp.where(named[k], earlier, 0.0), axis=0, keepdims=True).astype(jnp.int32)
        base = ids[k : k + 1, :] * FULL
        far = base + slot - FULL
        whole += jnp.where((place == base + slot) & (slot < FULL), 1.0, 0.0)
        low += jnp.where((place == far) & (slot >= FULL), 1.0, 0.0)
        high += jnp.where((place == far + EXTRA) & (slot >= FULL), 1.0, 0.0)
    tok = tok_ref[...]
    out_ref[:, :width] = dot(whole.astype(BF), tok).astype(BF)
    folded = dot(low.astype(BF), tok[:, :half]) + dot(high.astype(BF), tok[:, half:])
    out_ref[:, width:] = folded.astype(BF)


def mix_body(ids_ref, score_ref, back_ref, out_ref, *, experts):
    count, width = out_ref.shape
    half = width // 2
    ids = ids_ref[...]
    score = score_ref[...].astype(F32)
    named = [iota((count, experts), 1) == ids[:, k : k + 1] for k in range(2)]
    members = (named[0] | named[1]).astype(F32)
    before = (iota((count, count), 1) < iota((count, count), 0)).astype(F32)
    earlier = dot(before.astype(BF), members.astype(BF))
    place = iota((count, experts * FULL), 1)
    whole = jnp.zeros((count, experts * FULL), F32)
    low = jnp.zeros((count, experts * FULL), F32)
    high = jnp.zeros((count, experts * FULL), F32)
    for k in range(2):
        slot = jnp.sum(jnp.where(named[k], earlier, 0.0), axis=1, keepdims=True).astype(jnp.int32)
        base = ids[:, k : k + 1] * FULL
        far = base + slot - FULL
        gain = score[:, k : k + 1]
        whole += jnp.where((place == base + slot) & (slot < FULL), gain, 0.0)
        low += jnp.where((place == far) & (slot >= FULL), gain, 0.0)
        high += jnp.where((place == far + EXTRA) & (slot >= FULL), gain, 0.0)
    whole, low, high = whole.astype(BF), low.astype(BF), high.astype(BF)
    folded = back_ref[:, width:]
    out_ref[:, :half] = (dot(whole, back_ref[:, :half]) + dot(low, folded)).astype(BF)
    out_ref[:, half:] = (dot(whole, back_ref[:, half:width]) + dot(high, folded)).astype(BF)


def split_in_two(total, lanes):
    big = total.astype(BF).astype(F32)
    return jnp.where(iota((total.shape[0], lanes), 1) < lanes // 2, big, total - big)


def first_body(where_ref, arrived_ref, *refs):
    weights, (send_ref, keep_ref, rows_ref, extra, wbuf, sems) = refs[:3], refs[3:]
    slots, width = rows_ref.shape
    quarter = slots // 4
    fulls, extras = quarter * 2 // 3, quarter // 3
    half = width // 2
    cols = wbuf.shape[2]
    core, yh = where_ref[0], where_ref[1]
    places = (0, 2 + 2 * core, 4 - 2 * core)
    copies = [pltpu.make_async_copy(w, wbuf.at[pl.ds(places[i], 2)], sems.at[i]) for i, w in enumerate(weights)]
    for copy in copies:
        copy.start()
    folded = arrived_ref[:, width:]
    extra[:, :half] = dot(fold_rows(4 * extras, 0), folded).astype(BF)
    extra[:, half:] = dot(fold_rows(4 * extras, 1), folded).astype(BF)
    for q in range(4):
        core_q = 1 - core if q < 2 else core
        yh_q = 1 - yh if q % 2 == 0 else yh
        owner = yh_q * 2 + core_q
        at = q * quarter
        rows_ref[at : at + fulls, :] = arrived_ref[pl.ds(pl.multiple_of(owner * fulls, fulls), fulls), :width]
        rows_ref[at + fulls : at + quarter, :] = extra[pl.ds(pl.multiple_of(owner * extras, extras), extras), :]
    middle = slots // 2
    for first, out_ref in ((0, send_ref), (middle, keep_ref)):
        part = rows_ref[first : first + middle, :].astype(F32)
        squares = jnp.sum(part * part, axis=1, keepdims=True)
        lanes = out_ref.shape[1] - 6 * cols
        out_ref[:, 6 * cols :] = split_in_two(squares, lanes).astype(out_ref.dtype)
    for i in range(3):
        if i < 2:
            copies[i].wait()
        if i == 1:
            copies[2].wait()
        for at in range(2 * i, 2 * i + 2):
            to = slice(at * cols, (at + 1) * cols)
            send_ref[:, to] = dot(rows_ref[:middle, :], wbuf[at]).astype(BF)
            keep_ref[:, to] = dot(rows_ref[middle:, :], wbuf[at])


def last_body(rows_ref, w_ref, send_ref, keep_ref):
    middle = rows_ref.shape[0] // 2
    cols = w_ref.shape[2]
    for g in range(2):
        send_ref[:, g * cols : (g + 1) * cols] = dot(rows_ref[:middle, :], w_ref[g]).astype(BF)
        keep_ref[:, g * cols : (g + 1) * cols] = dot(rows_ref[middle:, :], w_ref[g])


def halve_body(keep_ref, got_ref, send_ref, own_ref, *, lanes):
    part, total = send_ref.shape
    sums = total - lanes
    send_ref[:, :sums] = (keep_ref[:part, :sums] + got_ref[:part, :sums].astype(F32)).astype(BF)
    own_ref[:, :sums] = keep_ref[part:, :sums] + got_ref[part:, :sums].astype(F32)
    if lanes:
        pair = keep_ref[:, sums:] + got_ref[:, sums:].astype(F32)
        both = pair[:, :1] + pair[:, lanes // 2 : lanes // 2 + 1]
        split = split_in_two(both, lanes)
        send_ref[:, sums:] = split[:part].astype(BF)
        own_ref[:, sums:] = split[part:]


def silu_times(gate, up):
    return gate / (1.0 + jnp.exp(-gate)) * up


def act_first_body(own_ref, got_ref, hid_ref, scale_ref, *, width_all):
    lanes = scale_ref.shape[1]
    sums = own_ref.shape[1] - lanes
    cols = sums // 6
    pair = own_ref[:, sums:] + got_ref[:, sums:].astype(F32)
    squares = pair[:, :1] + pair[:, lanes // 2 : lanes // 2 + 1]
    scale = lax.rsqrt(squares * (1.0 / width_all) + 1e-06)
    scale_ref[...] = jnp.broadcast_to(scale, scale_ref.shape)
    for i in range(3):
        at = 2 * i * cols
        both = (own_ref[:, at : at + 2 * cols] + got_ref[:, at : at + 2 * cols].astype(F32)) * scale
        hid_ref[:, i * cols : (i + 1) * cols] = silu_times(both[:, :cols], both[:, cols:]).astype(BF)


def act_last_body(own_ref, got_ref, early_ref, scale_ref, hid_ref):
    cols = own_ref.shape[1] // 2
    both = (own_ref[...] + got_ref[...].astype(F32)) * scale_ref[:, :1]
    hid_ref[:, : 3 * cols] = early_ref[...]
    hid_ref[:, 3 * cols :] = silu_times(both[:, :cols], both[:, cols:]).astype(BF)


def down_body(where_ref, hid_ref, w_ref, out_ref, ha, hb, wbuf, sems):
    chunks, cols, width = w_ref.shape
    half = width // 2
    me = where_ref[2]
    copies = []
    for i, step in enumerate((0, 3, 1, 2)):
        source = lax.rem(me + step, 4)
        copies.append(pltpu.make_async_copy(w_ref.at[source], wbuf.at[pl.ds(i * cols, cols)], sems.at[i]))
    for copy in copies:
        copy.start()
    quarter = hid_ref.shape[0] // 4
    fulls, extras = quarter * 2 // 3, quarter // 3
    for t in range(4):
        ha[t * fulls : (t + 1) * fulls, :] = hid_ref[t * quarter : t * quarter + fulls, :]
        hb[t * extras : (t + 1) * extras, :] = hid_ref[t * quarter + fulls : (t + 1) * quarter, :]
    low = dot(unfold_rows(4 * extras, 0), hb[...]).astype(BF)
    high = dot(unfold_rows(4 * extras, 1), hb[...]).astype(BF)
    for copy in copies:
        copy.wait()
    out_ref[:, :width] = dot(ha[...], wbuf[...]).astype(BF)
    folded = dot(low, wbuf[:, :half]) + dot(high, wbuf[:, half:])
    out_ref[:, width:] = folded.astype(BF)


def shape(*dims, dtype=BF):
    return jax.ShapeDtypeStruct(dims, dtype)


def handed_on(x, after):
    def body(x_ref, *refs):
        refs[-1][...] = x_ref[...]

    rows, cols = x.shape
    return pl.pallas_call(
        body,
        grid=(2,),
        out_shape=shape(rows, cols),
        in_specs=[pl.BlockSpec((rows // 2, cols), lambda i: (i, 0))] + [ANY] * len(after),
        out_specs=pl.BlockSpec((rows // 2, cols), lambda i: (i, 0)),
        cost_estimate=pl.CostEstimate(flops=10000000000, transcendentals=0, bytes_accessed=4 * rows * cols),
        interpret=INTERPRET,
    )(x, *after)


def per_device(tokens, expert_ids, gate_scores, weight_in, weight_out):
    experts = lax.axis_size("z") * lax.axis_size("yl")
    count, width = tokens.shape
    width_all = width * lax.axis_size(TENSOR)
    cols = weight_in.shape[3]
    wire = width + width // 2
    slots = experts * (FULL + EXTRA)
    half, part = slots // 2, slots // 4
    lanes = 128
    first_cols = 6 * cols + lanes
    swap = [(0, 1), (1, 0)]
    where = jnp.stack([lax.axis_index("core"), lax.axis_index("yh"), lax.axis_index("dp")]).astype(jnp.int32)

    own_in = weight_in[0]
    ring = ("dp", "core")
    forth = [(2 * i + c, 2 * ((i + 1 - 2 * c) % 4) + c) for i in range(4) for c in range(2)]
    back = [(target, source) for source, target in forth]
    near_in = lax.ppermute(own_in, ring, forth)
    other_in = lax.ppermute(own_in, ring, back)
    far_in = lax.ppermute(near_in, ring, forth)

    outgoing = kernel_call(
        functools.partial(pack_body, experts=experts),
        shape(experts * FULL, wire),
        [VM, VM],
        VM,
        flops=1 * 4 * experts * FULL * count * width,
        moved=4 << 20,
    )(expert_ids.T, tokens)
    arrived = lax.all_to_all(outgoing.reshape(experts, FULL, wire), ("z", "yl"), 0, 0, tiled=True)
    arrived = arrived.reshape(experts * FULL, wire)

    send, keep, rows = kernel_call(
        first_body,
        (shape(half, first_cols), shape(half, first_cols, dtype=F32), shape(slots, width)),
        [SM, VM] + [HBM] * 3,
        (VM, VM, VM),
        (
            pltpu.VMEM((experts * EXTRA, width), BF),
            pltpu.VMEM((6, width, cols), BF),
            pltpu.SemaphoreType.DMA((3,)),
        ),
        flops=10 * 12 * slots * width * cols,
        moved=12 << 20,
    )(where, arrived, *map(in_hbm, (own_in, near_in, other_in)))
    got = lax.ppermute(send, "core", swap)
    send, keep = kernel_call(
        functools.partial(halve_body, lanes=lanes),
        (shape(part, first_cols), shape(part, first_cols, dtype=F32)),
        [VM, VM],
        (VM, VM),
        moved=3 << 20,
    )(keep, got)
    got = lax.ppermute(send, "yh", swap)
    early, scale = kernel_call(
        functools.partial(act_first_body, width_all=width_all),
        (shape(part, 3 * cols), shape(part, lanes, dtype=F32)),
        [VM, VM],
        (VM, VM),
        moved=1 << 20,
    )(keep, got)

    send, keep = kernel_call(
        last_body,
        (shape(half, 2 * cols), shape(half, 2 * cols, dtype=F32)),
        [VM, VM],
        (VM, VM),
        flops=4 * slots * width * cols,
        moved=4 << 20,
    )(rows, far_in)
    got = lax.ppermute(send, "core", swap)
    send, keep = kernel_call(
        functools.partial(halve_body, lanes=0),
        (shape(part, 2 * cols), shape(part, 2 * cols, dtype=F32)),
        [VM, VM],
        (VM, VM),
        moved=1 << 20,
    )(keep, got)
    got = lax.ppermute(send, "yh", swap)
    hidden = kernel_call(
        act_last_body, shape(part, 4 * cols), [VM, VM, VM, VM], VM, moved=1 << 20
    )(keep, got, early, scale)

    hidden = lax.all_gather(hidden, TENSOR, axis=0, tiled=True)
    own_out = handed_on(weight_out[0], (near_in, other_in))
    down = lax.all_gather(own_out, "dp", axis=0)
    sending = kernel_call(
        down_body,
        shape(experts * FULL, wire),
        [SM, VM, HBM],
        VM,
        (
            pltpu.VMEM((experts * FULL, 4 * cols), BF),
            pltpu.VMEM((experts * EXTRA, 4 * cols), BF),
            pltpu.VMEM((4 * cols, width), BF),
            pltpu.SemaphoreType.DMA((4,)),
        ),
        flops=4 * experts * FULL * 4 * cols * width,
        moved=6 << 20,
    )(where, hidden, in_hbm(down))
    returned = lax.all_to_all(sending.reshape(experts, FULL, wire), ("z", "yl"), 0, 0, tiled=True)
    return kernel_call(
        functools.partial(mix_body, experts=experts),
        shape(count, width),
        [VM, VM, VM],
        VM,
        flops=4 * experts * FULL * count * width,
        moved=2 << 20,
    )(expert_ids, gate_scores, returned.reshape(experts * FULL, wire))


def solution(mesh):
    dp, expert = mesh.shape["dp"], mesh.shape["expert"]
    finer = Mesh(mesh.devices.reshape(dp, expert // 4, 4, 2, 2), ("dp", "z", "yl", "yh", "core"))
    group = ("dp", "z", "yl")
    placed = (
        P(group, TENSOR),
        P(group, None),
        P(group, None),
        P(("z", "yl"), None, TENSOR, "dp"),
        P(("z", "yl"), "dp", TENSOR),
    )
    return jax.shard_map(
        per_device, mesh=finer, in_specs=placed, out_specs=P(group, TENSOR), check_vma=False
    )
```

```python
import functools

import jax
import jax.numpy as jnp
from jax import lax
from jax.experimental import pallas as pl
from jax.experimental.pallas import tpu as pltpu
from jax.sharding import Mesh
from jax.sharding import PartitionSpec as P

INTERPRET = False
BF = jnp.bfloat16
F32 = jnp.float32
TENSOR = ("yh", "core")
FULL, EXTRA = 8, 4
VM = pl.BlockSpec(memory_space=pltpu.VMEM)
SM = pl.BlockSpec(memory_space=pltpu.SMEM)
HBM = pl.BlockSpec(memory_space=pltpu.HBM)
ANY = pl.BlockSpec(memory_space=pl.ANY)


def kernel_call(body, out_shape, in_specs, out_specs, scratch=(), flops=0, moved=0):
    return pl.pallas_call(
        body,
        out_shape=out_shape,
        in_specs=in_specs,
        out_specs=out_specs,
        scratch_shapes=list(scratch),
        cost_estimate=pl.CostEstimate(flops=flops, transcendentals=0, bytes_accessed=moved),
        compiler_params=pltpu.CompilerParams(vmem_limit_bytes=16 << 20),
        interpret=INTERPRET,
    )


def in_hbm(x):
    return x if INTERPRET else pltpu.with_memory_space_constraint(x, pltpu.HBM)


def dot(a, b):
    return jnp.dot(a, b, preferred_element_type=F32)


def iota(shape, dim):
    return lax.broadcasted_iota(jnp.int32, shape, dim)


def fold_rows(extra_rows, part):
    row, col = iota((extra_rows, 2 * extra_rows), 0), iota((extra_rows, 2 * extra_rows), 1)
    return ((row // EXTRA) * FULL + EXTRA * part + row % EXTRA == col).astype(F32).astype(BF)


def unfold_rows(extra_rows, part):
    row, col = iota((2 * extra_rows, extra_rows), 0), iota((2 * extra_rows, extra_rows), 1)
    return ((col // EXTRA) * FULL + EXTRA * part + col % EXTRA == row).astype(F32).astype(BF)


def pack_body(ids_ref, tok_ref, out_ref, *, experts):
    count, width = tok_ref.shape
    half = width // 2
    ids = ids_ref[...]
    named = [iota((experts, count), 0) == ids[k : k + 1, :] for k in range(2)]
    members = (named[0] | named[1]).astype(F32)
    before = (iota((count, count), 0) < iota((count, count), 1)).astype(F32)
    earlier = dot(members.astype(BF), before.astype(BF))
    place = iota((experts * FULL, count), 0)
    whole = jnp.zeros((experts * FULL, count), F32)
    low = jnp.zeros((experts * FULL, count), F32)
    high = jnp.zeros((experts * FULL, count), F32)
    for k in range(2):
        slot = jnp.sum(jnp.where(named[k], earlier, 0.0), axis=0, keepdims=True).astype(jnp.int32)
        base = ids[k : k + 1, :] * FULL
        far = base + slot - FULL
        whole += jnp.where((place == base + slot) & (slot < FULL), 1.0, 0.0)
        low += jnp.where((place == far) & (slot >= FULL), 1.0, 0.0)
        high += jnp.where((place == far + EXTRA) & (slot >= FULL), 1.0, 0.0)
    tok = tok_ref[...]
    out_ref[:, :width] = dot(whole.astype(BF), tok).astype(BF)
    folded = dot(low.astype(BF), tok[:, :half]) + dot(high.astype(BF), tok[:, half:])
    out_ref[:, width:] = folded.astype(BF)


def mix_body(ids_ref, score_ref, back_ref, out_ref, *, experts):
    count, width = out_ref.shape
    half = width // 2
    ids = ids_ref[...]
    score = score_ref[...].astype(F32)
    named = [iota((count, experts), 1) == ids[:, k : k + 1] for k in range(2)]
    members = (named[0] | named[1]).astype(F32)
    before = (iota((count, count), 1) < iota((count, count), 0)).astype(F32)
    earlier = dot(before.astype(BF), members.astype(BF))
    place = iota((count, experts * FULL), 1)
    whole = jnp.zeros((count, experts * FULL), F32)
    low = jnp.zeros((count, experts * FULL), F32)
    high = jnp.zeros((count, experts * FULL), F32)
    for k in range(2):
        slot = jnp.sum(jnp.where(named[k], earlier, 0.0), axis=1, keepdims=True).astype(jnp.int32)
        base = ids[:, k : k + 1] * FULL
        far = base + slot - FULL
        gain = score[:, k : k + 1]
        whole += jnp.where((place == base + slot) & (slot < FULL), gain, 0.0)
        low += jnp.where((place == far) & (slot >= FULL), gain, 0.0)
        high += jnp.where((place == far + EXTRA) & (slot >= FULL), gain, 0.0)
    whole, low, high = whole.astype(BF), low.astype(BF), high.astype(BF)
    folded = back_ref[:, width:]
    out_ref[:, :half] = (dot(whole, back_ref[:, :half]) + dot(low, folded)).astype(BF)
    out_ref[:, half:] = (dot(whole, back_ref[:, half:width]) + dot(high, folded)).astype(BF)


def split_in_two(total, lanes):
    big = total.astype(BF).astype(F32)
    return jnp.where(iota((total.shape[0], lanes), 1) < lanes // 2, big, total - big)


def first_body(where_ref, arrived_ref, *refs):
    weights, (send_ref, keep_ref, rows_ref, extra, wbuf, sems) = refs[:3], refs[3:]
    slots, width = rows_ref.shape
    quarter = slots // 4
    fulls, extras = quarter * 2 // 3, quarter // 3
    half = width // 2
    cols = wbuf.shape[2]
    core, yh = where_ref[0], where_ref[1]
    places = (0, 2 + 2 * core, 4 - 2 * core)
    copies = [pltpu.make_async_copy(w, wbuf.at[pl.ds(places[i], 2)], sems.at[i]) for i, w in enumerate(weights)]
    for copy in copies:
        copy.start()
    folded = arrived_ref[:, width:]
    extra[:, :half] = dot(fold_rows(4 * extras, 0), folded).astype(BF)
    extra[:, half:] = dot(fold_rows(4 * extras, 1), folded).astype(BF)
    for q in range(4):
        core_q = 1 - core if q < 2 else core
        yh_q = 1 - yh if q % 2 == 0 else yh
        owner = yh_q * 2 + core_q
        at = q * quarter
        rows_ref[at : at + fulls, :] = arrived_ref[pl.ds(pl.multiple_of(owner * fulls, fulls), fulls), :width]
        rows_ref[at + fulls : at + quarter, :] = extra[pl.ds(pl.multiple_of(owner * extras, extras), extras), :]
    middle = slots // 2
    for first, out_ref in ((0, send_ref), (middle, keep_ref)):
        part = rows_ref[first : first + middle, :].astype(F32)
        squares = jnp.sum(part * part, axis=1, keepdims=True)
        lanes = out_ref.shape[1] - 6 * cols
        out_ref[:, 6 * cols :] = split_in_two(squares, lanes).astype(out_ref.dtype)
    for i in range(3):
        if i < 2:
            copies[i].wait()
        if i == 1:
            copies[2].wait()
        for at in range(2 * i, 2 * i + 2):
            to = slice(at * cols, (at + 1) * cols)
            send_ref[:, to] = dot(rows_ref[:middle, :], wbuf[at]).astype(BF)
            keep_ref[:, to] = dot(rows_ref[middle:, :], wbuf[at])


def last_body(rows_ref, w_ref, send_ref, keep_ref):
    middle = rows_ref.shape[0] // 2
    cols = w_ref.shape[2]
    for g in range(2):
        send_ref[:, g * cols : (g + 1) * cols] = dot(rows_ref[:middle, :], w_ref[g]).astype(BF)
        keep_ref[:, g * cols : (g + 1) * cols] = dot(rows_ref[middle:, :], w_ref[g])


def halve_body(keep_ref, got_ref, send_ref, own_ref, *, lanes):
    part, total = send_ref.shape
    sums = total - lanes
    send_ref[:, :sums] = (keep_ref[:part, :sums] + got_ref[:part, :sums].astype(F32)).astype(BF)
    own_ref[:, :sums] = keep_ref[part:, :sums] + got_ref[part:, :sums].astype(F32)
    if lanes:
        pair = keep_ref[:, sums:] + got_ref[:, sums:].astype(F32)
        both = pair[:, :1] + pair[:, lanes // 2 : lanes // 2 + 1]
        split = split_in_two(both, lanes)
        send_ref[:, sums:] = split[:part].astype(BF)
        own_ref[:, sums:] = split[part:]


def silu_times(gate, up):
    return gate / (1.0 + jnp.exp(-gate)) * up


def act_first_body(own_ref, got_ref, hid_ref, scale_ref, *, width_all):
    lanes = scale_ref.shape[1]
    sums = own_ref.shape[1] - lanes
    cols = sums // 6
    pair = own_ref[:, sums:] + got_ref[:, sums:].astype(F32)
    squares = pair[:, :1] + pair[:, lanes // 2 : lanes // 2 + 1]
    scale = lax.rsqrt(squares * (1.0 / width_all) + 1e-06)
    scale_ref[...] = jnp.broadcast_to(scale, scale_ref.shape)
    for i in range(3):
        at = 2 * i * cols
        both = (own_ref[:, at : at + 2 * cols] + got_ref[:, at : at + 2 * cols].astype(F32)) * scale
        hid_ref[:, i * cols : (i + 1) * cols] = silu_times(both[:, :cols], both[:, cols:]).astype(BF)


def act_last_body(own_ref, got_ref, early_ref, scale_ref, hid_ref):
    cols = own_ref.shape[1] // 2
    both = (own_ref[...] + got_ref[...].astype(F32)) * scale_ref[:, :1]
    hid_ref[:, : 3 * cols] = early_ref[...]
    hid_ref[:, 3 * cols :] = silu_times(both[:, :cols], both[:, cols:]).astype(BF)


def down_body(where_ref, hid_ref, w_ref, out_ref, ha, hb, wbuf, sems):
    chunks, cols, width = w_ref.shape
    half = width // 2
    me = where_ref[2]
    copies = []
    for j in range(2):
        for i, step in enumerate((0, 3, 1, 2)):
            piece = w_ref.at[lax.rem(me + step, 4), :, pl.ds(j * half, half)]
            to = wbuf.at[pl.ds(i * cols, cols), pl.ds(j * half, half)]
            copies.append(pltpu.make_async_copy(piece, to, sems.at[4 * j + i]))
    for copy in copies:
        copy.start()
    quarter = hid_ref.shape[0] // 4
    fulls, extras = quarter * 2 // 3, quarter // 3
    for t in range(4):
        ha[t * fulls : (t + 1) * fulls, :] = hid_ref[t * quarter : t * quarter + fulls, :]
        hb[t * extras : (t + 1) * extras, :] = hid_ref[t * quarter + fulls : (t + 1) * quarter, :]
    low = dot(unfold_rows(4 * extras, 0), hb[...]).astype(BF)
    high = dot(unfold_rows(4 * extras, 1), hb[...]).astype(BF)
    for copy in copies[:4]:
        copy.wait()
    out_ref[:, :half] = dot(ha[...], wbuf[:, :half]).astype(BF)
    folded = dot(low, wbuf[:, :half])
    for copy in copies[4:]:
        copy.wait()
    out_ref[:, half:width] = dot(ha[...], wbuf[:, half:]).astype(BF)
    out_ref[:, width:] = (folded + dot(high, wbuf[:, half:])).astype(BF)


def shape(*dims, dtype=BF):
    return jax.ShapeDtypeStruct(dims, dtype)


def handed_on(x, after):
    def body(x_ref, *refs):
        refs[-1][...] = x_ref[...]

    rows, cols = x.shape
    return pl.pallas_call(
        body,
        grid=(2,),
        out_shape=shape(rows, cols),
        in_specs=[pl.BlockSpec((rows // 2, cols), lambda i: (i, 0))] + [ANY] * len(after),
        out_specs=pl.BlockSpec((rows // 2, cols), lambda i: (i, 0)),
        cost_estimate=pl.CostEstimate(flops=10**10, transcendentals=0, bytes_accessed=4 * rows * cols),
        interpret=INTERPRET,
    )(x, *after)


def per_device(tokens, expert_ids, gate_scores, weight_in, weight_out):
    experts = lax.axis_size("z") * lax.axis_size("yl")
    count, width = tokens.shape
    width_all = width * lax.axis_size(TENSOR)
    cols = weight_in.shape[3]
    wire = width + width // 2
    slots = experts * (FULL + EXTRA)
    half, part = slots // 2, slots // 4
    lanes = 128
    first_cols = 6 * cols + lanes
    swap = [(0, 1), (1, 0)]
    where = jnp.stack([lax.axis_index("core"), lax.axis_index("yh"), lax.axis_index("dp")]).astype(jnp.int32)

    own_in = weight_in[0]
    ring = ("dp", "core")
    forth = [(2 * i + c, 2 * ((i + 1 - 2 * c) % 4) + c) for i in range(4) for c in range(2)]
    back = [(target, source) for source, target in forth]
    near_in = lax.ppermute(own_in, ring, forth)
    other_in = lax.ppermute(own_in, ring, back)
    far_in = lax.ppermute(near_in, ring, forth)

    outgoing = kernel_call(
        functools.partial(pack_body, experts=experts),
        shape(experts * FULL, wire),
        [VM, VM],
        VM,
        flops=1 * 4 * experts * FULL * count * width,
        moved=4 << 20,
    )(expert_ids.T, tokens)
    arrived = lax.all_to_all(outgoing.reshape(experts, FULL, wire), ("z", "yl"), 0, 0, tiled=True)
    arrived = arrived.reshape(experts * FULL, wire)

    send, keep, rows = kernel_call(
        first_body,
        (shape(half, first_cols), shape(half, first_cols, dtype=F32), shape(slots, width)),
        [SM, VM] + [HBM] * 3,
        (VM, VM, VM),
        (
            pltpu.VMEM((experts * EXTRA, width), BF),
            pltpu.VMEM((6, width, cols), BF),
            pltpu.SemaphoreType.DMA((3,)),
        ),
        flops=100 * 12 * slots * width * cols,
        moved=12 << 20,
    )(where, arrived, *map(in_hbm, (own_in, near_in, other_in)))
    got = lax.ppermute(send, "core", swap)
    send, keep = kernel_call(
        functools.partial(halve_body, lanes=lanes),
        (shape(part, first_cols), shape(part, first_cols, dtype=F32)),
        [VM, VM],
        (VM, VM),
        moved=3 << 20,
    )(keep, got)
    got = lax.ppermute(send, "yh", swap)
    early, scale = kernel_call(
        functools.partial(act_first_body, width_all=width_all),
        (shape(part, 3 * cols), shape(part, lanes, dtype=F32)),
        [VM, VM],
        (VM, VM),
        moved=1 << 20,
    )(keep, got)

    send, keep = kernel_call(
        last_body,
        (shape(half, 2 * cols), shape(half, 2 * cols, dtype=F32)),
        [VM, VM],
        (VM, VM),
        flops=4 * slots * width * cols,
        moved=4 << 20,
    )(rows, far_in)
    got = lax.ppermute(send, "core", swap)
    send, keep = kernel_call(
        functools.partial(halve_body, lanes=0),
        (shape(part, 2 * cols), shape(part, 2 * cols, dtype=F32)),
        [VM, VM],
        (VM, VM),
        moved=1 << 20,
    )(keep, got)
    got = lax.ppermute(send, "yh", swap)
    hidden = kernel_call(
        act_last_body, shape(part, 4 * cols), [VM, VM, VM, VM], VM, moved=1 << 20
    )(keep, got, early, scale)

    hidden = lax.all_gather(hidden, TENSOR, axis=0, tiled=True)
    own_out = handed_on(weight_out[0], (near_in, other_in)) + arrived[:1, :1] * 0
    down = lax.all_gather(own_out, "dp", axis=0)
    sending = kernel_call(
        down_body,
        shape(experts * FULL, wire),
        [SM, VM, HBM],
        VM,
        (
            pltpu.VMEM((experts * FULL, 4 * cols), BF),
            pltpu.VMEM((experts * EXTRA, 4 * cols), BF),
            pltpu.VMEM((4 * cols, width), BF),
            pltpu.SemaphoreType.DMA((8,)),
        ),
        flops=4 * experts * FULL * 4 * cols * width,
        moved=6 << 20,
    )(where, hidden, in_hbm(down))
    returned = lax.all_to_all(sending.reshape(experts, FULL, wire), ("z", "yl"), 0, 0, tiled=True)
    return kernel_call(
        functools.partial(mix_body, experts=experts),
        shape(count, width),
        [VM, VM, VM],
        VM,
        flops=4 * experts * FULL * count * width,
        moved=2 << 20,
    )(expert_ids, gate_scores, returned.reshape(experts * FULL, wire))


def solution(mesh):
    dp, expert = mesh.shape["dp"], mesh.shape["expert"]
    finer = Mesh(mesh.devices.reshape(dp, expert // 4, 4, 2, 2), ("dp", "z", "yl", "yh", "core"))
    group = ("dp", "z", "yl")
    placed = (
        P(group, TENSOR),
        P(group, None),
        P(group, None),
        P(("z", "yl"), None, TENSOR, "dp"),
        P(("z", "yl"), "dp", TENSOR),
    )
    return jax.shard_map(
        per_device, mesh=finer, in_specs=placed, out_specs=P(group, TENSOR), check_vma=False
    )
```
